512 devices in a mesh: label: 64 (over z, x_hi, core), doc: 8 (over y, x_lo).
Axes of the slice: x: 4 (x_hi: 2, x_lo: 2; x = x_hi * 2 + x_lo), y: 4, z: 16, core: 2. Of those that a mesh axis runs over, the one named last changes fastest.
Arguments:
- tokens: bfloat16 [512, 128, 768], P(('label', 'doc')), may hold values from -6 to 6
- norm_gains: float32 [2, 768], replicated, may hold values from 0.1 to 1.9
- enc_weight: bfloat16 [768, 768], replicated, may hold values from -0.21875 to 0.21875
- head_weight: bfloat16 [262144, 768], P(('label', 'doc')), may hold values from -0.59765625 to 0.59765625
- head_bias: bfloat16 [262144], P(('label', 'doc')), may hold values from -12 to -7
- positives: int32 [512, 8], P(('label', 'doc')), may hold values from -1 to 262143, as said below
Outputs:
- row_grad: float32 [512, 768], P(('label', 'doc'))
- weight_grad: float32 [768, 768], replicated
- gain_grads: float32 [2, 768], replicated
The draws below stay inside these ranges and needn't reach their ends.
Inputs may be any that keep to these rules, and one draw needn't show every extreme that they name: `positives`: each document lists 3 to 8 label ids at the front of its row and -1 in the remaining slots; an id may repeat within a row and then counts once.
All inputs are finite; a program needn't handle non-finite values.
Results may differ from the reference program's by a relative error of at most 0.0025.
The reference program's roundings to bfloat16 on the way (of `act_in`, `embed_bf` and `d_logit`) count: a program that leaves them out, or rounds other values in their place, can miss the bound.
Values may be sent and summed in bfloat16 or wider, within the bound.
A program may use at most 64 MiB of HBM per device.

```python
import jax
import jax.numpy as jnp
from jax import lax

D = 768
SEQ = 128
DOC_DEV = 1
L_STORE = 512
POS = 8
DOCS = 512
LABELS = 262144
N_LABEL = 64
N_DOC = 8


def draw_positives(key, part):
    count_key, label_key = jax.random.split(jax.random.fold_in(key, 17))
    counts = jax.random.randint(count_key, (DOCS, 1), 3, POS + 1)
    label_ids = jax.random.randint(label_key, (DOCS, POS), 0, LABELS)
    slots = jnp.arange(POS)[None, :]
    return jnp.where(slots < counts, label_ids, -1).astype(jnp.int32)


def shard_levels(rng, dims, cuts, smallest, largest):
    def one(axis_at, parts):
        draws = jax.random.uniform(jax.random.fold_in(jax.random.fold_in(rng, 6), axis_at), (parts,), jnp.float32, smallest / len(cuts), largest / len(cuts))
        return jnp.repeat(jnp.exp(draws), dims[axis_at] // parts).reshape((-1,) + (1,) * (len(dims) - axis_at - 1))

    level = one(*cuts[0])
    for cut in cuts[1:]:
        level = level * one(*cut)
    return level


def gaussian(key, dims, scale, bound, pieces=(), kind=jnp.bfloat16):
    array = scale * jax.random.normal(key, dims, jnp.float32)
    if pieces:
        array = array * shard_levels(key, dims, pieces, -0.22, 0.18)
    return jnp.clip(array, -bound, bound).astype(kind)


def setup_inputs(seed: int = 0) -> dict:
    seeds = jax.random.split(jax.random.key(seed), 7)
    return {
        "tokens": gaussian(seeds[0], (DOCS, SEQ, D), 1.0, 6.0, ((0, 512),)),
        "norm_gains": jnp.clip(1.0 + 0.18 * jax.random.normal(seeds[1], (2, D), jnp.float32), 0.1, 1.9),
        "enc_weight": gaussian(seeds[2], (D, D), D ** -0.5, 0.21875),
        "head_weight": gaussian(seeds[3], (LABELS, D), 0.1, 0.59765625, ((0, 512),)),
        "head_bias": jnp.clip(-12.0 + 5.0 * jax.random.uniform(seeds[4], (LABELS,), jnp.float32) ** shard_levels(seeds[4], (LABELS,), ((0, 512),), -0.2, 0.2), -12.0, -7.0).astype(jnp.bfloat16),
        "positives": draw_positives(jax.random.fold_in(seeds[6], 71), 0),
    }


epsilon = 1e-05

def normalize(values):
    center = values - lax.optimization_barrier(jnp.mean(values, axis=-1, keepdims=True))
    inverse = lax.rsqrt(lax.optimization_barrier(jnp.mean(center * center, axis=-1, keepdims=True)) + epsilon)
    return (center * inverse, inverse)

def encode(tok_block, gains, enc_weight):
    width = tok_block.shape[-1]
    tok_flat = tok_block.reshape(-1, width).astype(jnp.float32)
    normed_in, _ = normalize(tok_flat)
    act_in = (normed_in * gains[0]).astype(jnp.bfloat16)
    pre_act = jnp.dot(act_in, enc_weight, preferred_element_type=jnp.float32)
    hidden = tok_flat + jax.nn.gelu(pre_act)
    pooled = lax.optimization_barrier(jnp.mean(hidden.reshape(tok_block.shape[0], tok_block.shape[1], width), axis=1))
    normed_out, inv_out = normalize(pooled)
    return (normed_out * gains[1], (normed_in, act_in, pre_act, normed_out, inv_out))

def encode_back(cotangent, saved, gains, enc_weight, seq_len):
    normed_in, act_in, pre_act, normed_out, inv_out = saved
    gain_out_grad = lax.optimization_barrier(jnp.sum(cotangent * normed_out, axis=0))
    d_normed = cotangent * gains[1]
    d_pooled = inv_out * (d_normed - lax.optimization_barrier(jnp.mean(d_normed, axis=-1, keepdims=True)) - normed_out * lax.optimization_barrier(jnp.mean(d_normed * normed_out, axis=-1, keepdims=True)))
    spread_grad = jnp.broadcast_to((d_pooled / seq_len)[:, None, :], (d_pooled.shape[0], seq_len, d_pooled.shape[1])).reshape(pre_act.shape)
    _, gelu_back = jax.vjp(jax.nn.gelu, pre_act)
    d_pre = gelu_back(spread_grad)[0]
    weight_grad = lax.dot_general(act_in.astype(jnp.float32), d_pre, (((0,), (0,)), ((), ())), precision=lax.Precision.HIGHEST, preferred_element_type=jnp.float32)
    d_act = lax.dot_general(d_pre, enc_weight.astype(jnp.float32), (((1,), (1,)), ((), ())), precision=lax.Precision.HIGHEST, preferred_element_type=jnp.float32)
    gain_in_grad = lax.optimization_barrier(jnp.sum(d_act * normed_in, axis=0))
    return (weight_grad, jnp.stack([gain_in_grad, gain_out_grad]))

def head_block(embed_bf, label_lists, weight_block, bias_block, first_label):
    logits = lax.dot_general(embed_bf, weight_block, (((1,), (1,)), ((), ())), preferred_element_type=jnp.float32)
    logits = logits + bias_block.astype(jnp.float32)[None, :]
    label_ids = first_label + jnp.arange(weight_block.shape[0], dtype=jnp.int32)
    target = jnp.any(label_lists[:, :, None] == label_ids[None, None, :], axis=1).astype(jnp.float32)
    d_logit = (jax.nn.sigmoid(logits) - target).astype(jnp.bfloat16)
    return jnp.dot(d_logit, weight_block, preferred_element_type=jnp.float32)

def reference(tokens, norm_gains, enc_weight, head_weight, head_bias, positives):
    tok_blocks = tokens.reshape(N_LABEL * N_DOC, DOC_DEV, SEQ, D)
    embed = lax.map(lambda tok_block: encode(tok_block, norm_gains, enc_weight)[0], tok_blocks).reshape(DOCS, D)
    embed_bf = embed.astype(jnp.bfloat16)
    span = L_STORE * N_DOC
    weight_blocks = head_weight.reshape(N_LABEL, span, D)
    bias_blocks = head_bias.reshape(N_LABEL, span)

    def add_block(total, inputs):
        block_index, weight_block, bias_block = inputs
        first_label = (block_index * span).astype(jnp.int32)
        return (total + head_block(embed_bf, positives, weight_block, bias_block, first_label), None)
    row_grad, _ = lax.scan(add_block, jnp.zeros((DOCS, D), jnp.float32), (jnp.arange(N_LABEL, dtype=jnp.int32), weight_blocks, bias_blocks))
    cotangent = row_grad

    def back_block(carry, inputs):
        tok_block, cot_block = inputs
        _, saved = encode(tok_block, norm_gains, enc_weight)
        weight_part, gain_part = encode_back(cot_block, saved, norm_gains, enc_weight, SEQ)
        return ((carry[0] + weight_part, carry[1] + gain_part), None)
    (weight_grad, gain_grads), _ = lax.scan(back_block, (jnp.zeros((D, D), jnp.float32), jnp.zeros((2, D), jnp.float32)), (tok_blocks, cotangent.reshape(N_LABEL * N_DOC, DOC_DEV, D)))
    return (row_grad, weight_grad, gain_grads)
```

```python
import math

import jax
import jax.numpy as jnp
from jax import lax
from jax.experimental import pallas as pl
from jax.experimental.pallas import tpu as pltpu
from jax.sharding import PartitionSpec as P

D, SEQ, SHARD = 768, 128, 512
NZ, NX, NY, NP = 16, 4, 4, 16
LANE, HALF, ROWS = 128, 384, 48
BLOCKS = D // LANE
EPSILON = 1e-05
BF16, F32 = jnp.bfloat16, jnp.float32
MESH = pl.DeviceIdType.MESH
ROOT = math.sqrt(2.0 / math.pi)
FAR_FIRST = (8, 7, 9, 6, 10, 5, 11, 4, 12, 3, 13, 2, 14, 1, 15)
COLUMNS = (0, 1, 3, 2)
PLANE = tuple(4 * dx + dy for dx in COLUMNS for dy in (1, 3, 2, 0) if dx or dy)


def device(z, x, y, c):
    return (z * 4 + lax.div(x, 2) * 2 + c, y * 2 + lax.rem(x, 2))


def contract(a, b, dims):
    return lax.dot_general(a, b, ((dims[:1], dims[1:]), ((), ())), preferred_element_type=F32)


def high_low(v):
    high = v.astype(BF16)
    return high, (v - high.astype(F32)).astype(BF16)


def kernel(
    tok_ref, gains_ref, enc_ref, head_ref, bias_ref, pos_ref,
    row_ref, grad_ref, gain_ref,
    head, bias2, act, gel, act2, gel2, bo, bp, pm, nrm, r8, g8, zs, zbuf, zf, xbuf,
    rs, rr, rown, rz, rzr, dpo, dpp, ws, wr, wown, gs1, gr1, s2, s2r, s3r, g2r, g3r, gfin, gfin2,
    local_sem, pair_send, pair_recv, za_s, za_r, xa_s, xa_r, xr_s, xr_r, zr_s, zr_r,
    w1_s, w1_r, g1_s, g1_r, w2_s, w2_r, g2_s, g2_r, w3_s, w3_r, g3_s, g3_r,
    w4_s, w4_r, w5_s, w5_r, g5_s, g5_r, w6_s, w6_r,
):
    label, doc = lax.axis_index("label"), lax.axis_index("doc")
    z, c = lax.div(label, 4), lax.rem(label, 2)
    x, y = lax.rem(lax.div(label, 2), 2) * 2 + lax.rem(doc, 2), lax.div(doc, 2)
    zh, zl = lax.div(z, 4), lax.rem(z, 4)
    me = x * 4 + y
    partner = device(z, x, y, 1 - c)

    def along(k):
        return device(lax.rem(z + k, NZ), x, y, c)

    def shifted(i):
        return lax.rem(x + i // 4, NX), lax.rem(y + i % 4, NY)

    def plane(i):
        return device(z, *shifted(i), c)

    def back(i):
        return (4 - i // 4) % 4 * 4 + (4 - i % 4) % 4

    def send(src, dst, send_sem, recv_sem, to):
        copy = pltpu.make_async_remote_copy(
            src_ref=src, dst_ref=dst, send_sem=send_sem, recv_sem=recv_sem, device_id=to, device_id_type=MESH
        )
        copy.start()
        return copy

    barrier = pltpu.get_barrier_semaphore()
    for to in [partner] + [along(k) for k in FAR_FIRST] + [plane(i) for i in PLANE]:
        pl.semaphore_signal(barrier, inc=1, device_id=to, device_id_type=MESH)
    own_head = pltpu.make_async_copy(head_ref, head.at[0], local_sem)
    own_head.start()

    tok = tok_ref[0].astype(F32)
    center = tok - jnp.mean(tok, axis=-1, keepdims=True)
    normed = center * lax.rsqrt(jnp.mean(center * center, axis=-1, keepdims=True) + EPSILON)
    nrm[...] = normed
    act[...] = (normed * gains_ref[0:1, :]).astype(BF16)
    pre = jnp.dot(act[...], enc_ref[...], preferred_element_type=F32)
    tanh = jnp.tanh(ROOT * (pre + 0.044715 * (pre * pre * pre)))
    cdf = 0.5 * (1.0 + tanh)
    pooled = jnp.mean(tok + pre * cdf, axis=0, keepdims=True)
    for b in range(BLOCKS):
        r8[b : b + 1, :] = pooled[:, b * LANE : (b + 1) * LANE]
        g8[b : b + 1, :] = gains_ref[1:2, b * LANE : (b + 1) * LANE]
    pooled = r8[0:BLOCKS, :]
    gain = g8[0:BLOCKS, :]
    center = pooled - jnp.sum(pooled) / D
    inverse = lax.rsqrt(jnp.sum(center * center, keepdims=True) / D + EPSILON)
    normed_out = center * inverse
    zs[...] = jnp.zeros_like(zs)
    zs[0:BLOCKS, :] = normed_out * gain
    ids = pos_ref[...]
    zs[6:7, 0:8] = (jnp.where(ids < 0, 512, jnp.right_shift(ids, 9)) - 256).astype(F32)
    zs[7:8, 0:8] = (jnp.bitwise_and(ids, 511) - 256).astype(F32)
    zbuf[0] = zs[...].astype(BF16)

    pl.semaphore_wait(barrier, 31)
    zgather = [send(zbuf.at[0], zbuf.at[k], za_s.at[k], za_r.at[k], along(k)) for k in FAR_FIRST]
    pair = [
        send(head_ref, head.at[1], pair_send.at[0], pair_recv.at[0], partner),
        send(bias_ref, bias2, pair_send.at[1], pair_recv.at[1], partner),
    ]

    slope = cdf + (0.5 * ROOT) * pre * (1.0 - tanh * tanh) * (1.0 + 0.134145 * (pre * pre))
    high, low = high_low(slope)
    for h in range(2):
        gel[h, 0] = high[:, h * HALF : (h + 1) * HALF]
        gel[h, 1] = low[:, h * HALF : (h + 1) * HALF]
    pair += [
        send(act, act2, pair_send.at[2], pair_recv.at[2], partner),
        send(gel.at[1 - c], gel2, pair_send.at[3], pair_recv.at[3], partner),
    ]
    for q in range(3):
        cols = slice(q * 256, (q + 1) * 256)
        n_high, n_low = high_low(nrm[:, cols])
        for h in range(2):
            block = contract(n_high, gel[h, 0], (0, 0)) + contract(n_low, gel[h, 0], (0, 0)) + contract(n_high, gel[h, 1], (0, 0))
            pm[cols, h * HALF : (h + 1) * HALF] = block * enc_ref[cols, h * HALF : (h + 1) * HALF].astype(F32)
    for ref in (rz, dpo, gs1):
        ref[...] = jnp.zeros_like(ref)

    for copy in zgather:
        copy.wait_recv()
    zf[...] = zbuf[...].reshape(NZ * 8, LANE).astype(F32)
    for b in range(BLOCKS):
        xbuf[0, :, b * LANE : (b + 1) * LANE] = zf[pl.ds(b, NZ, stride=8), :].astype(BF16)
    first, second = zf[pl.ds(6, NZ, stride=8), :], zf[pl.ds(7, NZ, stride=8), :]
    lanes = lax.broadcasted_iota(jnp.int32, (NZ, LANE), 1)
    xbuf[0, :, D:] = jnp.where(lanes < 8, first, pltpu.roll(second, 8, 1)).astype(BF16)
    xgather = {i: send(xbuf.at[0], xbuf.at[i], xa_s.at[i], xa_r.at[i], plane(i)) for i in PLANE}

    for copy in pair[2:]:
        copy.wait_recv()
    for q in range(3):
        cols = slice(q * 256, (q + 1) * 256)
        bo[cols, :] = contract(act[:, cols], gel[c, 0], (0, 0)) + contract(act[:, cols], gel[c, 1], (0, 0))
        bp[cols, :] = contract(act2[:, cols], gel2[0], (0, 0)) + contract(act2[:, cols], gel2[1], (0, 0))
    own_head.wait()
    for copy in pair[:2]:
        copy.wait_recv()

    flat = label * 8 + doc
    bases = (flat * SHARD, (flat + (1 - 2 * c) * 8) * SHARD)
    spots = lax.broadcasted_iota(jnp.int32, (64, SHARD), 1)
    xreduce = []
    for dx in COLUMNS:
        slots = [4 * dx + dy for dy in range(4)]
        for i in slots:
            if i:
                xgather[i].wait_recv()
        embed = xbuf[4 * dx : 4 * dx + 4, :, 0:D].reshape(64, D)
        code = xbuf[4 * dx : 4 * dx + 4, :, D:].reshape(64, LANE).astype(F32)
        ids = ((code + 256.0) * 512.0 + (pltpu.roll(code, LANE - 8, 1) + 256.0)).astype(jnp.int32)
        total = jnp.zeros((64, D), F32)
        for s in range(2):
            logits = contract(embed, head[s], (1, 1)) + (bias_ref, bias2)[s][...]
            near = ids - bases[s]
            target = near[:, 0:1] == spots
            for q in range(1, 8):
                target = jnp.logical_or(target, near[:, q : q + 1] == spots)
            d_logit = (jax.nn.sigmoid(logits) - target.astype(F32)).astype(BF16)
            total += jnp.dot(d_logit, head[s], preferred_element_type=F32)
        for dy, i in enumerate(slots):
            part = total[16 * dy : 16 * dy + 16]
            if i:
                rs[i] = part.astype(BF16)
            else:
                rown[...] = part
        for i in slots:
            if i:
                xreduce.append(send(rs.at[i], rr.at[i], xr_s.at[i], xr_r.at[i], plane(back(i))))
    for copy in xreduce:
        copy.wait_recv()
    total = rown[...]
    for i in range(1, NP):
        total += rr[i].astype(F32)
    for b in range(BLOCKS):
        rz[pl.ds(b, NZ, stride=8), :] = total[:, b * LANE : (b + 1) * LANE]
    zreduce = [
        send(rz.at[pl.ds(8 * k, 8), :], rzr.at[pl.ds(8 * k, 8), :], zr_s.at[k], zr_r.at[k], along(NZ - k))
        for k in FAR_FIRST
    ]
    for copy in zreduce:
        copy.wait_recv()
    rowg = rz[0:8, :]
    for k in range(1, NZ):
        rowg += rzr[8 * k : 8 * k + 8, :]

    cot = rowg[0:BLOCKS]
    d_normed = cot * gain
    d_pooled = inverse * (d_normed - jnp.sum(d_normed) / D - normed_out * (jnp.sum(d_normed * normed_out) / D))
    dpo[0:BLOCKS, :] = d_pooled / SEQ
    dcopy = send(dpo, dpp, pair_send.at[4], pair_recv.at[4], partner)
    for b in range(BLOCKS):
        row_ref[:, b * LANE : (b + 1) * LANE] = rowg[b : b + 1]
    dcopy.wait_recv()
    mine = jnp.concatenate([dpo[pl.ds(3 * c + b, 1), :] for b in range(3)], axis=1)
    theirs = jnp.concatenate([dpp[pl.ds(3 * c + b, 1), :] for b in range(3)], axis=1)

    def weight_block(spot):
        at = pl.ds(pl.multiple_of(spot * ROWS, 16), ROWS)
        return bo[at, :] * mine + bp[at, :] * theirs

    copies = []
    w1 = []
    for i in PLANE:
        px, py = shifted(i)
        ws[i] = weight_block(px * 4 + py).astype(BF16)
    for i in PLANE:
        w1.append(send(ws.at[i], wr.at[i], w1_s.at[i], w1_r.at[i], plane(i)))
    wown[...] = weight_block(me)
    lane_sum = pm[:, 0:LANE] * dpo[0:1, :]
    for b in range(1, BLOCKS):
        lane_sum += pm[:, b * LANE : (b + 1) * LANE] * dpo[b : b + 1, :]
    gain_in = lax.dot_general(
        jnp.ones((8, LANE), F32), lane_sum, (((1,), (1,)), ((), ())),
        precision=lax.Precision.HIGHEST, preferred_element_type=F32,
    )
    gain_out = cot * normed_out
    for b in range(BLOCKS):
        gs1[b] = gain_in[0:1, b * LANE : (b + 1) * LANE]
        gs1[BLOCKS + b] = gain_out[b : b + 1, :]
    g1 = []
    for i in PLANE:
        px, py = shifted(i)
        g1.append(send(gs1.at[px * 4 + py], gr1.at[i], g1_s.at[i], g1_r.at[i], plane(i)))
    for copy in w1:
        copy.wait_recv()
    total = wown[...]
    for i in range(1, NP):
        total += wr[i].astype(F32)
    for r in range(3):
        s2[r] = total[16 * r : 16 * r + 16]

    near_z = [lax.rem(zl + d, 4) for d in range(4)]
    from_z = [lax.rem(zl + 4 - d, 4) for d in range(4)]

    def cube(d):
        return device(zh * 4 + near_z[d], x, y, c)

    def cubes(d):
        return along(4 * d)

    def third(d):
        return pltpu.make_async_remote_copy(
            src_ref=s2.at[lax.rem(near_z[d], 3)], dst_ref=s2r.at[d], send_sem=w2_s.at[d], recv_sem=w2_r.at[d],
            device_id=cube(d), device_id_type=MESH,
        )

    for d in range(1, 4):
        pl.when(near_z[d] < 3)(lambda d=d: third(d).start())
    for copy in g1:
        copy.wait_recv()
    gsum = gs1[me]
    for i in range(1, NP):
        gsum += gr1[i]
    g2r[zl] = gsum
    g2 = [send(g2r.at[zl], g2r.at[zl], g2_s.at[d], g2_r.at[d], cube(d)) for d in range(1, 4)]

    def sum_across():
        part = s2[zl]
        for d in range(1, 4):
            third(d).wait_recv()
        for d in range(1, 4):
            part += s2r[d]
        s3r[zh] = part
        across = [send(s3r.at[zh], s3r.at[zh], w3_s.at[d], w3_r.at[d], cubes(d)) for d in range(1, 4)]
        for copy in across:
            copy.wait_recv()
        whole = s3r[0] + s3r[1] + s3r[2] + s3r[3]
        grad_ref[c, me, zl] = whole.astype(BF16)
        for copy in across:
            copy.wait_send()

    pl.when(zl < 3)(sum_across)

    def fourth(d):
        at = (c, me, lax.rem(zl, 3))
        return pltpu.make_async_remote_copy(
            src_ref=grad_ref.at[at], dst_ref=grad_ref.at[at], send_sem=w4_s.at[d], recv_sem=w4_r.at[d],
            device_id=cube(d), device_id_type=MESH,
        )

    def spread():
        for d in range(1, 4):
            fourth(d).start()

    pl.when(zl < 3)(spread)
    for copy in g2:
        copy.wait_recv()
    g3r[zh] = g2r[0] + g2r[1] + g2r[2] + g2r[3]
    g3 = [send(g3r.at[zh], g3r.at[zh], g3_s.at[d], g3_r.at[d], cubes(d)) for d in range(1, 4)]
    for d in range(1, 4):
        pl.when(from_z[d] < 3)(lambda d=d: fourth(d).wait_recv())

    w5 = {i: send(grad_ref.at[c, me], grad_ref.at[c, me], w5_s.at[i], w5_r.at[i], plane(i)) for i in PLANE}
    w6 = [send(grad_ref.at[c, me], grad_ref.at[c, me], w6_s.at[0], w6_r.at[0], partner)]
    for copy in g3:
        copy.wait_recv()
    gfin[me] = g3r[0] + g3r[1] + g3r[2] + g3r[3]
    g5 = [send(gfin.at[me], gfin.at[me], g5_s.at[i], g5_r.at[i], plane(i)) for i in PLANE]
    for i in PLANE:
        w5[i].wait_recv()
        px, py = shifted(back(i))
        at = (c, px * 4 + py)
        w6.append(send(grad_ref.at[at], grad_ref.at[at], w6_s.at[i], w6_r.at[i], partner))
    for copy in g5:
        copy.wait_recv()
    gcopy = send(gfin, gfin2, pair_send.at[5], pair_recv.at[5], partner)
    gcopy.wait_recv()
    for b in range(BLOCKS):
        gain_ref[0:1, b * LANE : (b + 1) * LANE] = gfin[b] + gfin2[b]
        gain_ref[1:2, b * LANE : (b + 1) * LANE] = gfin[BLOCKS + b] + gfin2[BLOCKS + b]
    for copy in w6:
        copy.wait_recv()
    for copy in [*zgather, *pair, *xgather.values(), *xreduce, *zreduce, dcopy, *w1, *g1, *g2, *g3, *w5.values(), *g5, *w6, gcopy]:
        copy.wait_send()
    for d in range(1, 4):
        pl.when(near_z[d] < 3)(lambda d=d: third(d).wait_send())

    def spread_sent():
        for d in range(1, 4):
            fourth(d).wait_send()

    pl.when(zl < 3)(spread_sent)


def shards(tokens, norm_gains, enc_weight, head_weight, head_bias, positives):
    vmem, dma = pltpu.VMEM, pltpu.SemaphoreType.DMA
    in_vmem, anywhere = pl.BlockSpec(memory_space=pltpu.VMEM), pl.BlockSpec(memory_space=pl.ANY)
    scratch = [
        vmem((2, SHARD, D), BF16),
        vmem((1, SHARD), F32),
        vmem((SEQ, D), BF16),
        vmem((2, 2, SEQ, HALF), BF16),
        vmem((SEQ, D), BF16),
        vmem((2, SEQ, HALF), BF16),
        vmem((D, HALF), F32),
        vmem((D, HALF), F32),
        vmem((D, D), F32),
        vmem((SEQ, D), F32),
        vmem((8, LANE), F32),
        vmem((8, LANE), F32),
        vmem((8, LANE), F32),
        vmem((NZ, 8, LANE), BF16),
        vmem((NZ * 8, LANE), F32),
        vmem((NP, NZ, D + LANE), BF16),
        vmem((NP, NZ, D), BF16),
        vmem((NP, NZ, D), BF16),
        vmem((NZ, D), F32),
        vmem((NZ * 8, LANE), F32),
        vmem((NZ * 8, LANE), F32),
        vmem((8, LANE), F32),
        vmem((8, LANE), F32),
        vmem((NP, ROWS, HALF), BF16),
        vmem((NP, ROWS, HALF), BF16),
        vmem((ROWS, HALF), F32),
        vmem((NP, 1, LANE), F32),
        vmem((NP, 1, LANE), F32),
        vmem((3, 16, HALF), F32),
        vmem((4, 16, HALF), F32),
        vmem((4, 16, HALF), F32),
        vmem((4, 1, LANE), F32),
        vmem((4, 1, LANE), F32),
        vmem((NP, 1, LANE), F32),
        vmem((NP, 1, LANE), F32),
        dma,
        dma((6,)), dma((6,)),
        dma((NZ,)), dma((NZ,)),
        dma((NP,)), dma((NP,)),
        dma((NP,)), dma((NP,)),
        dma((NZ,)), dma((NZ,)),
        dma((NP,)), dma((NP,)),
        dma((NP,)), dma((NP,)),
        dma((4,)), dma((4,)),
        dma((4,)), dma((4,)),
        dma((4,)), dma((4,)),
        dma((4,)), dma((4,)),
        dma((4,)), dma((4,)),
        dma((NP,)), dma((NP,)),
        dma((NP,)), dma((NP,)),
        dma((NP,)), dma((NP,)),
    ]
    row_grad, grad, gain_grads = pl.pallas_call(
        kernel,
        out_shape=(
            jax.ShapeDtypeStruct((1, D), F32),
            jax.ShapeDtypeStruct((2, NP, 3, 16, HALF), BF16),
            jax.ShapeDtypeStruct((2, D), F32),
        ),
        in_specs=[in_vmem, in_vmem, in_vmem, anywhere, in_vmem, in_vmem],
        out_specs=(in_vmem, in_vmem, in_vmem),
        scratch_shapes=scratch,
        compiler_params=pltpu.CompilerParams(collective_id=0, has_side_effects=True),
    )(tokens, norm_gains, enc_weight, head_weight, head_bias.astype(F32).reshape(1, SHARD), positives)
    halves = grad.reshape(2, D, HALF)
    weight_grad = jnp.concatenate([halves[0], halves[1]], axis=1).astype(F32)
    return (row_grad, weight_grad, gain_grads)


def solution(mesh):
    placed = (P(("label", "doc"), None, None), P(), P(), P(("label", "doc"), None), P(("label", "doc")), P(("label", "doc"), None))
    return jax.shard_map(
        shards, mesh=mesh, in_specs=placed, out_specs=(P(("label", "doc"), None), P(), P()), check_vma=False
    )
```

```python
import math

import jax
import jax.numpy as jnp
from jax import lax
from jax.experimental import pallas as pl
from jax.experimental.pallas import tpu as pltpu
from jax.sharding import PartitionSpec as P

D, SEQ, SHARD = 768, 128, 512
NZ, NX, NY, NP = 16, 4, 4, 16
LANE, HALF, ROWS = 128, 384, 48
BLOCKS = D // LANE
EPSILON = 1e-05
BF16, F32 = jnp.bfloat16, jnp.float32
MESH = pl.DeviceIdType.MESH
ROOT = math.sqrt(2.0 / math.pi)
FAR_FIRST = (8, 7, 9, 6, 10, 5, 11, 4, 12, 3, 13, 2, 14, 1, 15)
COLUMNS = (0, 1, 3, 2)
PLANE = tuple(4 * dx + dy for dx in COLUMNS for dy in (1, 3, 2, 0) if dx or dy)


def device(z, x, y, c):
    return (z * 4 + lax.div(x, 2) * 2 + c, y * 2 + lax.rem(x, 2))


def contract(a, b, dims):
    return lax.dot_general(a, b, ((dims[:1], dims[1:]), ((), ())), preferred_element_type=F32)


def high_low(v):
    high = v.astype(BF16)
    return high, (v - high.astype(F32)).astype(BF16)


def kernel(
    tok_hbm, gains_hbm, enc_hbm, head_hbm, bias_hbm, pos_hbm,
    row_ref, grad_ref, gain_ref,
    tok_ref, gains_ref, enc_ref, pos_ref, head, bias0, bias1, act, gel, act2, gel2, bo, bp, pm, nrm, r8, g8, zs, zbuf, zf, xbuf,
    rs, rr, rown, rz, rzr, dpo, dpp, ws, wr, wown, gs1, gs1p, gr1, s2, s2r, s3r, g2r, g3r, gfin,
    local_sem, pair_send, pair_recv, za_s, za_r, xa_s, xa_r, xr_s, xr_r, zr_s, zr_r,
    w1_s, w1_r, g1_s, g1_r, w2_s, w2_r, g2_s, g2_r, w3_s, w3_r, g3_s, g3_r,
    w4_s, w4_r, w5_s, w5_r, g5_s, g5_r, w6_s, w6_r,
):
    label, doc = lax.axis_index("label"), lax.axis_index("doc")
    z, c = lax.div(label, 4), lax.rem(label, 2)
    x, y = lax.rem(lax.div(label, 2), 2) * 2 + lax.rem(doc, 2), lax.div(doc, 2)
    zh, zl = lax.div(z, 4), lax.rem(z, 4)
    me = x * 4 + y
    partner = device(z, x, y, 1 - c)

    def along(k):
        return device(lax.rem(z + k, NZ), x, y, c)

    def shifted(i):
        return lax.rem(x + i // 4, NX), lax.rem(y + i % 4, NY)

    def plane(i):
        return device(z, *shifted(i), c)

    def back(i):
        return (4 - i // 4) % 4 * 4 + (4 - i % 4) % 4

    def send(src, dst, send_sem, recv_sem, to):
        copy = pltpu.make_async_remote_copy(
            src_ref=src, dst_ref=dst, send_sem=send_sem, recv_sem=recv_sem, device_id=to, device_id_type=MESH
        )
        copy.start()
        return copy

    local = [
        pltpu.make_async_copy(src, dst, local_sem.at[n])
        for n, (src, dst) in enumerate((
            (tok_hbm, tok_ref), (gains_hbm, gains_ref), (enc_hbm, enc_ref), (pos_hbm, pos_ref),
            (head_hbm, head.at[0]), (bias_hbm, bias0),
        ))
    ]
    for copy in local[:4]:
        copy.start()
    barrier = pltpu.get_barrier_semaphore()
    for to in [partner] + [along(k) for k in FAR_FIRST] + [plane(i) for i in PLANE]:
        pl.semaphore_signal(barrier, inc=1, device_id=to, device_id_type=MESH)

    for copy in local[4:]:
        copy.start()

    local[0].wait()
    local[1].wait()
    tok = tok_ref[0].astype(F32)
    center = tok - jnp.mean(tok, axis=-1, keepdims=True)
    normed = center * lax.rsqrt(jnp.mean(center * center, axis=-1, keepdims=True) + EPSILON)
    nrm[...] = normed
    act[...] = (normed * gains_ref[0:1, :]).astype(BF16)
    local[2].wait()
    pre = jnp.dot(act[...], enc_ref[...], preferred_element_type=F32)
    tanh = jnp.tanh(ROOT * (pre + 0.044715 * (pre * pre * pre)))
    cdf = 0.5 * (1.0 + tanh)
    pooled = jnp.mean(tok + pre * cdf, axis=0, keepdims=True)
    for b in range(BLOCKS):
        r8[b : b + 1, :] = pooled[:, b * LANE : (b + 1) * LANE]
        g8[b : b + 1, :] = gains_ref[1:2, b * LANE : (b + 1) * LANE]
    pooled = r8[0:BLOCKS, :]
    gain = g8[0:BLOCKS, :]
    center = pooled - jnp.sum(pooled) / D
    inverse = lax.rsqrt(jnp.sum(center * center, keepdims=True) / D + EPSILON)
    normed_out = center * inverse
    zs[...] = jnp.zeros_like(zs)
    zs[0:BLOCKS, :] = normed_out * gain
    local[3].wait()
    ids = pos_ref[...]
    zs[6:7, 0:8] = (jnp.where(ids < 0, 512, jnp.right_shift(ids, 9)) - 256).astype(F32)
    zs[7:8, 0:8] = (jnp.bitwise_and(ids, 511) - 256).astype(F32)
    zbuf[0] = zs[...].astype(BF16)

    pl.semaphore_wait(barrier, 31)
    zgather = [send(zbuf.at[0], zbuf.at[k], za_s.at[k], za_r.at[k], along(k)) for k in FAR_FIRST]
    pair = [
        send(head_hbm, head.at[1], pair_send.at[0], pair_recv.at[0], partner),
        send(bias_hbm, bias1, pair_send.at[1], pair_recv.at[1], partner),
    ]

    slope = cdf + (0.5 * ROOT) * pre * (1.0 - tanh * tanh) * (1.0 + 0.134145 * (pre * pre))
    high, low = high_low(slope)
    for h in range(2):
        gel[h, 0] = high[:, h * HALF : (h + 1) * HALF]
        gel[h, 1] = low[:, h * HALF : (h + 1) * HALF]
    pair += [
        send(act, act2, pair_send.at[2], pair_recv.at[2], partner),
        send(gel.at[1 - c], gel2, pair_send.at[3], pair_recv.at[3], partner),
    ]
    for q in range(3):
        cols = slice(q * 256, (q + 1) * 256)
        n_high, n_low = high_low(nrm[:, cols])
        for h in range(2):
            block = contract(n_high, gel[h, 0], (0, 0)) + contract(n_low, gel[h, 0], (0, 0)) + contract(n_high, gel[h, 1], (0, 0))
            pm[cols, h * HALF : (h + 1) * HALF] = block * enc_ref[cols, h * HALF : (h + 1) * HALF].astype(F32)
    for ref in (rz, dpo, gs1):
        ref[...] = jnp.zeros_like(ref)

    for copy in zgather:
        copy.wait_recv()
    zf[...] = zbuf[...].reshape(NZ * 8, LANE).astype(F32)
    for b in range(BLOCKS):
        xbuf[0, :, b * LANE : (b + 1) * LANE] = zf[pl.ds(b, NZ, stride=8), :].astype(BF16)
    first, second = zf[pl.ds(6, NZ, stride=8), :], zf[pl.ds(7, NZ, stride=8), :]
    lanes = lax.broadcasted_iota(jnp.int32, (NZ, LANE), 1)
    xbuf[0, :, D:] = jnp.where(lanes < 8, first, pltpu.roll(second, 8, 1)).astype(BF16)
    xgather = {i: send(xbuf.at[0], xbuf.at[i], xa_s.at[i], xa_r.at[i], plane(i)) for i in PLANE}

    for copy in pair[2:]:
        copy.wait_recv()
    for q in range(3):
        cols = slice(q * 256, (q + 1) * 256)
        bo[cols, :] = contract(act[:, cols], gel[c, 0], (0, 0)) + contract(act[:, cols], gel[c, 1], (0, 0))
        bp[cols, :] = contract(act2[:, cols], gel2[0], (0, 0)) + contract(act2[:, cols], gel2[1], (0, 0))
    local[4].wait()
    local[5].wait()
    for copy in pair[:2]:
        copy.wait_recv()

    flat = label * 8 + doc
    bases = (flat * SHARD, (flat + (1 - 2 * c) * 8) * SHARD)
    spots = lax.broadcasted_iota(jnp.int32, (64, SHARD), 1)
    xreduce = []
    for dx in COLUMNS:
        slots = [4 * dx + dy for dy in range(4)]
        for i in slots:
            if i:
                xgather[i].wait_recv()
        embed = xbuf[4 * dx : 4 * dx + 4, :, 0:D].reshape(64, D)
        code = xbuf[4 * dx : 4 * dx + 4, :, D:].reshape(64, LANE).astype(F32)
        ids = ((code + 256.0) * 512.0 + (pltpu.roll(code, LANE - 8, 1) + 256.0)).astype(jnp.int32)
        total = jnp.zeros((64, D), F32)
        for s in range(2):
            logits = contract(embed, head[s], (1, 1)) + (bias0, bias1)[s][...].astype(F32).reshape(1, SHARD)
            near = ids - bases[s]
            target = near[:, 0:1] == spots
            for q in range(1, 8):
                target = jnp.logical_or(target, near[:, q : q + 1] == spots)
            d_logit = (jax.nn.sigmoid(logits) - target.astype(F32)).astype(BF16)
            total += jnp.dot(d_logit, head[s], preferred_element_type=F32)
        for dy, i in enumerate(slots):
            part = total[16 * dy : 16 * dy + 16]
            if i:
                rs[i] = part.astype(BF16)
            else:
                rown[...] = part
        for i in slots:
            if i:
                xreduce.append(send(rs.at[i], rr.at[i], xr_s.at[i], xr_r.at[i], plane(back(i))))
    for copy in xreduce:
        copy.wait_recv()
    total = rown[...]
    for i in range(1, NP):
        total += rr[i].astype(F32)
    for b in range(BLOCKS):
        rz[pl.ds(b, NZ, stride=8), :] = total[:, b * LANE : (b + 1) * LANE]
    zreduce = [
        send(rz.at[pl.ds(8 * k, 8), :], rzr.at[pl.ds(8 * k, 8), :], zr_s.at[k], zr_r.at[k], along(NZ - k))
        for k in FAR_FIRST
    ]
    for copy in zreduce:
        copy.wait_recv()
    rowg = rz[0:8, :]
    for k in range(1, NZ):
        rowg += rzr[8 * k : 8 * k + 8, :]

    cot = rowg[0:BLOCKS]
    d_normed = cot * gain
    d_pooled = inverse * (d_normed - jnp.sum(d_normed) / D - normed_out * (jnp.sum(d_normed * normed_out) / D))
    dpo[0:BLOCKS, :] = d_pooled / SEQ
    dcopy = send(dpo, dpp, pair_send.at[4], pair_recv.at[4], partner)
    for b in range(BLOCKS):
        row_ref[:, b * LANE : (b + 1) * LANE] = rowg[b : b + 1]
    dcopy.wait_recv()
    mine = jnp.concatenate([dpo[pl.ds(3 * c + b, 1), :] for b in range(3)], axis=1)
    theirs = jnp.concatenate([dpp[pl.ds(3 * c + b, 1), :] for b in range(3)], axis=1)

    def weight_block(spot, r):
        at = pl.ds(pl.multiple_of(spot * ROWS + 16 * r, 16), 16)
        return bo[at, :] * mine + bp[at, :] * theirs

    w1 = {}
    for r in range(3):
        for i in PLANE:
            px, py = shifted(i)
            ws[i, r] = weight_block(px * 4 + py, r).astype(BF16)
        for i in PLANE:
            w1[i, r] = send(ws.at[i, r], wr.at[i, r], w1_s.at[3 * i + r], w1_r.at[3 * i + r], plane(i))
    for r in range(3):
        wown[r] = weight_block(me, r)
    lane_sum = pm[:, 0:LANE] * dpo[0:1, :]
    for b in range(1, BLOCKS):
        lane_sum += pm[:, b * LANE : (b + 1) * LANE] * dpo[b : b + 1, :]
    gain_in = lax.dot_general(
        jnp.ones((8, LANE), F32), lane_sum, (((1,), (1,)), ((), ())),
        precision=lax.Precision.HIGHEST, preferred_element_type=F32,
    )
    gain_out = cot * normed_out
    for b in range(BLOCKS):
        gs1[b] = gain_in[0:1, b * LANE : (b + 1) * LANE]
        gs1[BLOCKS + b] = gain_out[b : b + 1, :]
    gcopy = send(gs1, gs1p, pair_send.at[5], pair_recv.at[5], partner)
    gcopy.wait_recv()
    g3r[...] = gs1[...] + gs1p[...]
    g1 = []
    for i in PLANE:
        px, py = shifted(i)
        g1.append(send(g3r.at[px * 4 + py], gr1.at[i], g1_s.at[i], g1_r.at[i], plane(i)))

    near_z = [lax.rem(zl + d, 4) for d in range(4)]

    def cube(d):
        return device(zh * 4 + near_z[d], x, y, c)

    def cubes(d):
        return along(4 * d)

    def piece(spot, r):
        rows = pl.ds(pl.multiple_of(spot * ROWS + 16 * r, 16), 16)
        return grad_ref.at[rows, pl.ds(pl.multiple_of(c * HALF, LANE), HALF)]

    def second(r):
        d = lax.rem(r + 4 - zl, 4)
        return pltpu.make_async_remote_copy(
            src_ref=s2.at[r], dst_ref=s2r.at[d], send_sem=w2_s.at[r], recv_sem=w2_r.at[d],
            device_id=device(zh * 4 + r, x, y, c), device_id_type=MESH,
        )

    def landed(d):
        return pltpu.make_async_remote_copy(
            src_ref=s2r.at[d], dst_ref=s2r.at[d], send_sem=w2_s.at[0], recv_sem=w2_r.at[d],
            device_id=cube(d), device_id_type=MESH,
        )

    def across(d):
        return pltpu.make_async_remote_copy(
            src_ref=s3r.at[zh], dst_ref=s3r.at[zh], send_sem=w3_s.at[d], recv_sem=w3_r.at[d],
            device_id=cubes(d), device_id_type=MESH,
        )

    def fourth(d, r):
        return pltpu.make_async_remote_copy(
            src_ref=piece(me, r), dst_ref=piece(me, r), send_sem=w4_s.at[d], recv_sem=w4_r.at[r],
            device_id=cube(d), device_id_type=MESH,
        )

    def start_across(r):
        for d in range(1, 4):
            landed(d).wait_recv()
        s3r[zh] = s2[r] + s2r[1] + s2r[2] + s2r[3]
        for d in range(1, 4):
            across(d).start()

    def end_across(r):
        for d in range(1, 4):
            across(d).wait_recv()
        whole = s3r[0] + s3r[1] + s3r[2] + s3r[3]
        piece(me, r)[...] = whole.astype(BF16)
        for d in range(1, 4):
            fourth(d, r).start()

    for r in range(3):
        for i in PLANE:
            w1[i, r].wait_recv()
        total = wown[r]
        for i in range(1, NP):
            total += wr[i, r].astype(F32)
        s2[r] = total
        pl.when(zl != r)(lambda r=r: second(r).start())
        if r == 1:
            pl.when(zl == 0)(lambda: start_across(0))
    pl.when(zl == 1)(lambda: start_across(1))
    pl.when(zl == 2)(lambda: start_across(2))
    for copy in g1:
        copy.wait_recv()
    gsum = g3r[me]
    for i in range(1, NP):
        gsum += gr1[i]
    g2r[zl] = gsum
    g2 = [send(g2r.at[zl], g2r.at[zl], g2_s.at[d], g2_r.at[d], cube(d)) for d in range(1, 4)]
    for copy in g2:
        copy.wait_recv()
    g2r[4 + zh] = g2r[0] + g2r[1] + g2r[2] + g2r[3]
    g3 = [send(g2r.at[4 + zh], g2r.at[4 + zh], g3_s.at[d], g3_r.at[d], cubes(d)) for d in range(1, 4)]

    w5, w6 = {}, []
    for r in range(3):
        if r == 2:
            for copy in g3:
                copy.wait_recv()
            gfin[me] = g2r[4] + g2r[5] + g2r[6] + g2r[7]
            g5 = [send(gfin.at[me], gfin.at[me], g5_s.at[i], g5_r.at[i], plane(i)) for i in PLANE]
        pl.when(zl == r)(lambda r=r: end_across(r))
        pl.when(zl != r)(lambda r=r: fourth(1, r).wait_recv())
        for i in PLANE:
            w5[i, r] = send(piece(me, r), piece(me, r), w5_s.at[3 * i + r], w5_r.at[3 * i + r], plane(i))
        w6.append(send(piece(me, r), piece(me, r), w6_s.at[r], w6_r.at[r], partner))
    for r in range(3):
        for i in PLANE:
            w5[i, r].wait_recv()
            px, py = shifted(back(i))
            at = piece(px * 4 + py, r)
            w6.append(send(at, at, w6_s.at[3 * i + r], w6_r.at[3 * i + r], partner))
    for copy in g5:
        copy.wait_recv()
    for b in range(BLOCKS):
        gain_ref[0:1, b * LANE : (b + 1) * LANE] = gfin[b]
        gain_ref[1:2, b * LANE : (b + 1) * LANE] = gfin[BLOCKS + b]
    for copy in w6:
        copy.wait_recv()
    for copy in [*zgather, *pair, *xgather.values(), *xreduce, *zreduce, dcopy, *w1.values(), gcopy, *g1, *g2, *g3, *w5.values(), *g5, *w6]:
        copy.wait_send()
    for r in range(3):
        pl.when(zl != r)(lambda r=r: second(r).wait_send())

    def sent():
        for d in range(1, 4):
            across(d).wait_send()
            fourth(d, 0).wait_send()

    pl.when(zl < 3)(sent)


def widen(grad_ref, row_ref, gain_ref, wide_ref, row_out, gain_out):
    wide_ref[...] = grad_ref[...].astype(F32)
    row_out[...] = row_ref[...]
    gain_out[...] = gain_ref[...]


def shards(tokens, norm_gains, enc_weight, head_weight, head_bias, positives):
    vmem, dma = pltpu.VMEM, pltpu.SemaphoreType.DMA
    in_vmem, anywhere = pl.BlockSpec(memory_space=pltpu.VMEM), pl.BlockSpec(memory_space=pl.ANY)
    scratch = [
        vmem((1, SEQ, D), BF16),
        vmem((2, D), F32),
        vmem((D, D), BF16),
        vmem((1, 8), jnp.int32),
        vmem((2, SHARD, D), BF16),
        vmem((SHARD,), BF16),
        vmem((SHARD,), BF16),
        vmem((SEQ, D), BF16),
        vmem((2, 2, SEQ, HALF), BF16),
        vmem((SEQ, D), BF16),
        vmem((2, SEQ, HALF), BF16),
        vmem((D, HALF), F32),
        vmem((D, HALF), F32),
        vmem((D, D), F32),
        vmem((SEQ, D), F32),
        vmem((8, LANE), F32),
        vmem((8, LANE), F32),
        vmem((8, LANE), F32),
        vmem((NZ, 8, LANE), BF16),
        vmem((NZ * 8, LANE), F32),
        vmem((NP, NZ, D + LANE), BF16),
        vmem((NP, NZ, D), BF16),
        vmem((NP, NZ, D), BF16),
        vmem((NZ, D), F32),
        vmem((NZ * 8, LANE), F32),
        vmem((NZ * 8, LANE), F32),
        vmem((8, LANE), F32),
        vmem((8, LANE), F32),
        vmem((NP, 3, 16, HALF), BF16),
        vmem((NP, 3, 16, HALF), BF16),
        vmem((3, 16, HALF), F32),
        vmem((NP, 1, LANE), F32),
        vmem((NP, 1, LANE), F32),
        vmem((NP, 1, LANE), F32),
        vmem((3, 16, HALF), F32),
        vmem((4, 16, HALF), F32),
        vmem((4, 16, HALF), F32),
        vmem((8, 1, LANE), F32),
        vmem((NP, 1, LANE), F32),
        vmem((NP, 1, LANE), F32),
        dma((6,)),
        dma((6,)), dma((6,)),
        dma((NZ,)), dma((NZ,)),
        dma((NP,)), dma((NP,)),
        dma((NP,)), dma((NP,)),
        dma((NZ,)), dma((NZ,)),
        dma((3 * NP,)), dma((3 * NP,)),
        dma((NP,)), dma((NP,)),
        dma((4,)), dma((4,)),
        dma((4,)), dma((4,)),
        dma((4,)), dma((4,)),
        dma((4,)), dma((4,)),
        dma((4,)), dma((4,)),
        dma((3 * NP,)), dma((3 * NP,)),
        dma((NP,)), dma((NP,)),
        dma((3 * NP,)), dma((3 * NP,)),
    ]
    row_grad, grad, gain_grads = pl.pallas_call(
        kernel,
        out_shape=(
            jax.ShapeDtypeStruct((1, D), F32),
            jax.ShapeDtypeStruct((D, D), BF16),
            jax.ShapeDtypeStruct((2, D), F32),
        ),
        in_specs=[anywhere] * 6,
        out_specs=(in_vmem, in_vmem, in_vmem),
        scratch_shapes=scratch,
        compiler_params=pltpu.CompilerParams(collective_id=0, has_side_effects=True),
    )(tokens, norm_gains, enc_weight, head_weight, head_bias, positives)
    small = [pl.BlockSpec((rows, D), lambda i: (0, 0)) for rows in (1, 2)]
    tile = pl.BlockSpec((D // 4, D), lambda i: (i, 0))
    weight_grad, row_grad, gain_grads = pl.pallas_call(
        widen,
        grid=(4,),
        out_shape=tuple(jax.ShapeDtypeStruct((rows, D), F32) for rows in (D, 1, 2)),
        in_specs=[tile, *small],
        out_specs=(tile, *small),
    )(grad, row_grad, gain_grads)
    return (row_grad, weight_grad, gain_grads)


def solution(mesh):
    placed = (P(("label", "doc"), None, None), P(), P(), P(("label", "doc"), None), P(("label", "doc")), P(("label", "doc"), None))
    return jax.shard_map(
        shards, mesh=mesh, in_specs=placed, out_specs=(P(("label", "doc"), None), P(), P()), check_vma=False
    )
```

```python
import math

import jax
import jax.numpy as jnp
from jax import lax
from jax.experimental import pallas as pl
from jax.experimental.pallas import tpu as pltpu
from jax.sharding import PartitionSpec as P

D, SEQ, SHARD = 768, 128, 512
NZ, NX, NY, NP = 16, 4, 4, 16
LANE, HALF, ROWS = 128, 384, 48
BLOCKS = D // LANE
EPSILON = 1e-05
BF16, F32 = jnp.bfloat16, jnp.float32
MESH = pl.DeviceIdType.MESH
ROOT = math.sqrt(2.0 / math.pi)
STEP = (0, 1, 2, 3, 13, 14, 15, 4, 5, 6, 7, 8, 9, 10, 11, 12)
FAR_FIRST = (11, 10, 12, 9, 13, 8, 14, 15, 7, 3, 4, 2, 5, 1, 6)
PAIRS = ((0, 1), (3, 2))
PLANE = tuple(4 * dx + dy for pair in PAIRS for dx in pair for dy in (1, 3, 2, 0) if dx or dy)


def device(z, x, y, c):
    return (z * 4 + lax.div(x, 2) * 2 + c, y * 2 + lax.rem(x, 2))


def contract(a, b, dims):
    return lax.dot_general(a, b, ((dims[:1], dims[1:]), ((), ())), preferred_element_type=F32)


def high_low(v):
    high = v.astype(BF16)
    return high, (v - high.astype(F32)).astype(BF16)


def kernel(
    tok_hbm, gains_hbm, enc_hbm, head_hbm, bias_hbm, pos_hbm,
    row_ref, grad_ref, gain_ref,
    tok_ref, gains_ref, enc_ref, pos_ref, head, bias0, bias1, act, gel, act2, gel2, bo, bp, pm, nrm, r8, g8, zs, zbuf, zf, xbuf,
    rs, rr, rown, rz, rzr, dpo, dpp, ws, wr, wown, gs1, gs1p, gr1, s2, s2r, s3r, g2r, g3r, gfin, half, rowout,
    local_sem, pair_send, pair_recv, za_s, za_r, xa_s, xa_r, xr_s, xr_r, zr_s, zr_r,
    w1_s, w1_r, g1_s, g1_r, w2_s, w2_r, g2_s, g2_r, w3_s, w3_r, g3_s, g3_r,
    w4_s, w4_r, w5_s, w5_r, g5_s, g5_r, w6_s, w6_r,
):
    label, doc = lax.axis_index("label"), lax.axis_index("doc")
    z, c = lax.div(label, 4), lax.rem(label, 2)
    x, y = lax.rem(lax.div(label, 2), 2) * 2 + lax.rem(doc, 2), lax.div(doc, 2)
    zh, zl = lax.div(z, 4), lax.rem(z, 4)
    me = x * 4 + y
    partner = device(z, x, y, 1 - c)

    def along(k):
        return device(lax.rem(z + k, NZ), x, y, c)

    def shifted(i):
        return lax.rem(x + i // 4, NX), lax.rem(y + i % 4, NY)

    def plane(i):
        return device(z, *shifted(i), c)

    def back(i):
        return (4 - i // 4) % 4 * 4 + (4 - i % 4) % 4

    def send(src, dst, send_sem, recv_sem, to):
        copy = pltpu.make_async_remote_copy(
            src_ref=src, dst_ref=dst, send_sem=send_sem, recv_sem=recv_sem, device_id=to, device_id_type=MESH
        )
        copy.start()
        return copy

    local = [
        pltpu.make_async_copy(src, dst, local_sem.at[n])
        for n, (src, dst) in enumerate((
            (tok_hbm, tok_ref), (gains_hbm, gains_ref), (enc_hbm, enc_ref), (pos_hbm, pos_ref),
            (head_hbm, head.at[0]), (bias_hbm, bias0),
        ))
    ]
    for copy in local[:4]:
        copy.start()
    barrier = pltpu.get_barrier_semaphore()
    for to in [partner] + [along(STEP[k]) for k in FAR_FIRST] + [plane(i) for i in PLANE]:
        pl.semaphore_signal(barrier, inc=1, device_id=to, device_id_type=MESH)

    for copy in local[4:]:
        copy.start()

    local[0].wait()
    local[1].wait()
    tok = tok_ref[0].astype(F32)
    center = tok - jnp.mean(tok, axis=-1, keepdims=True)
    normed = center * lax.rsqrt(jnp.mean(center * center, axis=-1, keepdims=True) + EPSILON)
    nrm[...] = normed
    act[...] = (normed * gains_ref[0:1, :]).astype(BF16)
    local[2].wait()
    pre = jnp.dot(act[...], enc_ref[...], preferred_element_type=F32)
    tanh = jnp.tanh(ROOT * (pre + 0.044715 * (pre * pre * pre)))
    cdf = 0.5 * (1.0 + tanh)
    pooled = jnp.mean(tok + pre * cdf, axis=0, keepdims=True)
    for b in range(BLOCKS):
        r8[b : b + 1, :] = pooled[:, b * LANE : (b + 1) * LANE]
        g8[b : b + 1, :] = gains_ref[1:2, b * LANE : (b + 1) * LANE]
    pooled = r8[0:BLOCKS, :]
    gain = g8[0:BLOCKS, :]
    center = pooled - jnp.sum(pooled) / D
    inverse = lax.rsqrt(jnp.sum(center * center, keepdims=True) / D + EPSILON)
    normed_out = center * inverse
    zs[...] = jnp.zeros_like(zs)
    zs[0:BLOCKS, :] = normed_out * gain
    local[3].wait()
    ids = pos_ref[...]
    zs[6:7, 0:8] = (jnp.where(ids < 0, 512, jnp.right_shift(ids, 9)) - 256).astype(F32)
    zs[7:8, 0:8] = (jnp.bitwise_and(ids, 511) - 256).astype(F32)
    zbuf[0] = zs[...].astype(BF16)

    pl.semaphore_wait(barrier, 31)
    zgather = {k: send(zbuf.at[0], zbuf.at[k], za_s.at[k], za_r.at[k], along(STEP[k])) for k in FAR_FIRST}
    pair = [
        send(head_hbm, head.at[1], pair_send.at[0], pair_recv.at[0], partner),
        send(bias_hbm, bias1, pair_send.at[1], pair_recv.at[1], partner),
    ]

    slope = cdf + (0.5 * ROOT) * pre * (1.0 - tanh * tanh) * (1.0 + 0.134145 * (pre * pre))
    high, low = high_low(slope)
    for h in range(2):
        gel[h, 0] = high[:, h * HALF : (h + 1) * HALF]
        gel[h, 1] = low[:, h * HALF : (h + 1) * HALF]
    pair += [
        send(act, act2, pair_send.at[2], pair_recv.at[2], partner),
        send(gel.at[1 - c], gel2, pair_send.at[3], pair_recv.at[3], partner),
    ]
    for q in range(3):
        cols = slice(q * 256, (q + 1) * 256)
        n_high, n_low = high_low(nrm[:, cols])
        for h in range(2):
            block = contract(n_high, gel[h, 0], (0, 0)) + contract(n_low, gel[h, 0], (0, 0)) + contract(n_high, gel[h, 1], (0, 0))
            pm[cols, h * HALF : (h + 1) * HALF] = block * enc_ref[cols, h * HALF : (h + 1) * HALF].astype(F32)
    for ref in (rz, dpo, gs1):
        ref[...] = jnp.zeros_like(ref)

    xgather = {}
    for h in range(2):
        for k in range(8 * h, 8 * h + 8):
            if k:
                zgather[k].wait_recv()
        zf[64 * h : 64 * h + 64, :] = zbuf[8 * h : 8 * h + 8].reshape(64, LANE).astype(F32)
        for b in range(BLOCKS):
            xbuf[0, h, :, b * LANE : (b + 1) * LANE] = zf[pl.ds(64 * h + b, 8, stride=8), :].astype(BF16)
        first, second = zf[pl.ds(64 * h + 6, 8, stride=8), :], zf[pl.ds(64 * h + 7, 8, stride=8), :]
        lanes = lax.broadcasted_iota(jnp.int32, (8, LANE), 1)
        xbuf[0, h, :, D:] = jnp.where(lanes < 8, first, pltpu.roll(second, 8, 1)).astype(BF16)
        for i in PLANE:
            at = 2 * i + h
            xgather[i, h] = send(xbuf.at[0, h], xbuf.at[i, h], xa_s.at[at], xa_r.at[at], plane(i))

    for copy in pair[2:]:
        copy.wait_recv()
    for q in range(3):
        cols = slice(q * 256, (q + 1) * 256)
        bo[cols, :] = contract(act[:, cols], gel[c, 0], (0, 0)) + contract(act[:, cols], gel[c, 1], (0, 0))
        bp[cols, :] = contract(act2[:, cols], gel2[0], (0, 0)) + contract(act2[:, cols], gel2[1], (0, 0))
    local[4].wait()
    local[5].wait()
    for copy in pair[:2]:
        copy.wait_recv()

    flat = label * 8 + doc
    bases = (flat * SHARD, (flat + (1 - 2 * c) * 8) * SHARD)
    spots = lax.broadcasted_iota(jnp.int32, (64, SHARD), 1)
    xreduce = {}
    for h, columns in [(h, columns) for h in range(2) for columns in PAIRS]:
        slots = [4 * dx + dy for dx in columns for dy in range(4)]
        for i in slots:
            if i:
                xgather[i, h].wait_recv()
        block = jnp.concatenate([xbuf[4 * dx : 4 * dx + 4, h].reshape(32, D + LANE) for dx in columns], axis=0)
        embed = block[:, 0:D]
        code = block[:, D:].astype(F32)
        ids = ((code + 256.0) * 512.0 + (pltpu.roll(code, LANE - 8, 1) + 256.0)).astype(jnp.int32)
        total = jnp.zeros((64, D), F32)
        for s in range(2):
            logits = contract(embed, head[s], (1, 1)) + (bias0, bias1)[s][...].astype(F32).reshape(1, SHARD)
            near = ids - bases[s]
            target = near[:, 0:1] == spots
            for q in range(1, 8):
                target = jnp.logical_or(target, near[:, q : q + 1] == spots)
            d_logit = (jax.nn.sigmoid(logits) - target.astype(F32)).astype(BF16)
            total += jnp.dot(d_logit, head[s], preferred_element_type=F32)
        for m, i in enumerate(slots):
            part = total[8 * m : 8 * m + 8]
            if i:
                rs[i, h] = part.astype(BF16)
            else:
                rown[h] = part
        for i in slots:
            if i:
                at = 2 * i + h
                xreduce[i, h] = send(rs.at[i, h], rr.at[i, h], xr_s.at[at], xr_r.at[at], plane(back(i)))
    zreduce = []
    for h in range(2):
        for i in PLANE:
            xreduce[i, h].wait_recv()
        total = rown[h]
        for i in range(1, NP):
            total += rr[i, h].astype(F32)
        for b in range(BLOCKS):
            rz[pl.ds(64 * h + b, 8, stride=8), :] = total[:, b * LANE : (b + 1) * LANE]
        for k in FAR_FIRST:
            if k // 8 == h:
                at = pl.ds(8 * k, 8)
                zreduce.append(send(rz.at[at, :], rzr.at[at, :], zr_s.at[k], zr_r.at[k], along(NZ - STEP[k])))
    for copy in zreduce:
        copy.wait_recv()
    rowg = rz[0:8, :]
    for k in range(1, NZ):
        rowg += rzr[8 * k : 8 * k + 8, :]

    cot = rowg[0:BLOCKS]
    d_normed = cot * gain
    d_pooled = inverse * (d_normed - jnp.sum(d_normed) / D - normed_out * (jnp.sum(d_normed * normed_out) / D))
    dpo[0:BLOCKS, :] = d_pooled / SEQ
    dcopy = send(dpo, dpp, pair_send.at[4], pair_recv.at[4], partner)
    rowout[...] = rowg
    row_out = pltpu.make_async_copy(rowout, row_ref, local_sem.at[2])
    row_out.start()
    dcopy.wait_recv()
    mine = jnp.concatenate([dpo[pl.ds(3 * c + b, 1), :] for b in range(3)], axis=1)
    theirs = jnp.concatenate([dpp[pl.ds(3 * c + b, 1), :] for b in range(3)], axis=1)

    def weight_block(spot, r):
        at = pl.ds(pl.multiple_of(spot * ROWS + 16 * r, 16), 16)
        return bo[at, :] * mine + bp[at, :] * theirs

    w1 = {}
    for r in range(3):
        for i in PLANE:
            px, py = shifted(i)
            ws[i, r] = weight_block(px * 4 + py, r).astype(BF16)
        for i in PLANE:
            w1[i, r] = send(ws.at[i, r], wr.at[i, r], w1_s.at[3 * i + r], w1_r.at[3 * i + r], plane(i))
    for r in range(3):
        wown[r] = weight_block(me, r)
    lane_sum = pm[:, 0:LANE] * dpo[0:1, :]
    for b in range(1, BLOCKS):
        lane_sum += pm[:, b * LANE : (b + 1) * LANE] * dpo[b : b + 1, :]
    gain_in = lax.dot_general(
        jnp.ones((8, LANE), F32), lane_sum, (((1,), (1,)), ((), ())),
        precision=lax.Precision.HIGHEST, preferred_element_type=F32,
    )
    gain_out = cot * normed_out
    for b in range(BLOCKS):
        gs1[b] = gain_in[0:1, b * LANE : (b + 1) * LANE]
        gs1[BLOCKS + b] = gain_out[b : b + 1, :]
    gcopy = send(gs1, gs1p, pair_send.at[5], pair_recv.at[5], partner)
    gcopy.wait_recv()
    g3r[...] = gs1[...] + gs1p[...]
    g1 = []
    for i in PLANE:
        px, py = shifted(i)
        g1.append(send(g3r.at[px * 4 + py], gr1.at[i], g1_s.at[i], g1_r.at[i], plane(i)))

    near_z = [lax.rem(zl + d, 4) for d in range(4)]

    def cube(d):
        return device(zh * 4 + near_z[d], x, y, c)

    def cubes(d):
        return along(4 * d)

    def piece(spot, r):
        return half.at[pl.ds(pl.multiple_of(spot * ROWS + 16 * r, 16), 16), :]

    def placed(spot, r):
        rows = pl.ds(pl.multiple_of(spot * ROWS + 16 * r, 16), 16)
        return grad_ref.at[rows, pl.ds(pl.multiple_of(c * HALF, LANE), HALF)]

    def second(r):
        d = lax.rem(r + 4 - zl, 4)
        return pltpu.make_async_remote_copy(
            src_ref=s2.at[r], dst_ref=s2r.at[d], send_sem=w2_s.at[r], recv_sem=w2_r.at[d],
            device_id=device(zh * 4 + r, x, y, c), device_id_type=MESH,
        )

    def landed(d):
        return pltpu.make_async_remote_copy(
            src_ref=s2r.at[d], dst_ref=s2r.at[d], send_sem=w2_s.at[0], recv_sem=w2_r.at[d],
            device_id=cube(d), device_id_type=MESH,
        )

    def across(d):
        return pltpu.make_async_remote_copy(
            src_ref=s3r.at[zh], dst_ref=s3r.at[zh], send_sem=w3_s.at[d], recv_sem=w3_r.at[d],
            device_id=cubes(d), device_id_type=MESH,
        )

    def fourth(d, r):
        return pltpu.make_async_remote_copy(
            src_ref=piece(me, r), dst_ref=piece(me, r), send_sem=w4_s.at[d], recv_sem=w4_r.at[r],
            device_id=cube(d), device_id_type=MESH,
        )

    def start_across(r):
        for d in range(1, 4):
            landed(d).wait_recv()
        s3r[zh] = s2[r] + s2r[1] + s2r[2] + s2r[3]
        for d in range(1, 4):
            across(d).start()

    def end_across(r):
        for d in range(1, 4):
            across(d).wait_recv()
        whole = s3r[0] + s3r[1] + s3r[2] + s3r[3]
        piece(me, r)[...] = whole.astype(BF16)
        for d in range(1, 4):
            fourth(d, r).start()

    for r in range(3):
        for i in PLANE:
            w1[i, r].wait_recv()
        total = wown[r]
        for i in range(1, NP):
            total += wr[i, r].astype(F32)
        s2[r] = total
        pl.when(zl != r)(lambda r=r: second(r).start())
        if r == 1:
            pl.when(zl == 0)(lambda: start_across(0))
    pl.when(zl == 1)(lambda: start_across(1))
    pl.when(zl == 2)(lambda: start_across(2))
    for copy in g1:
        copy.wait_recv()
    gsum = g3r[me]
    for i in range(1, NP):
        gsum += gr1[i]
    g2r[zl] = gsum
    g2 = [send(g2r.at[zl], g2r.at[zl], g2_s.at[d], g2_r.at[d], cube(d)) for d in range(1, 4)]
    for copy in g2:
        copy.wait_recv()
    g2r[4 + zh] = g2r[0] + g2r[1] + g2r[2] + g2r[3]
    g3 = [send(g2r.at[4 + zh], g2r.at[4 + zh], g3_s.at[d], g3_r.at[d], cubes(d)) for d in range(1, 4)]

    w5, w6 = {}, []
    for r in range(3):
        if r == 2:
            for copy in g3:
                copy.wait_recv()
            gfin[me] = g2r[4] + g2r[5] + g2r[6] + g2r[7]
            g5 = [send(gfin.at[me], gfin.at[me], g5_s.at[i], g5_r.at[i], plane(i)) for i in PLANE]
        pl.when(zl == r)(lambda r=r: end_across(r))
        pl.when(zl != r)(lambda r=r: fourth(1, r).wait_recv())
        for i in PLANE:
            w5[i, r] = send(piece(me, r), piece(me, r), w5_s.at[3 * i + r], w5_r.at[3 * i + r], plane(i))
        w6.append(send(piece(me, r), placed(me, r), w6_s.at[r], w6_r.at[r], partner))
    for r in range(3):
        for i in PLANE:
            w5[i, r].wait_recv()
            px, py = shifted(back(i))
            spot = px * 4 + py
            w6.append(send(piece(spot, r), placed(spot, r), w6_s.at[3 * i + r], w6_r.at[3 * i + r], partner))
    own_half = pltpu.make_async_copy(half, grad_ref.at[:, pl.ds(pl.multiple_of(c * HALF, LANE), HALF)], local_sem.at[0])
    own_half.start()
    for copy in g5:
        copy.wait_recv()
    gains_out = pltpu.make_async_copy(gfin, gain_ref, local_sem.at[1])
    gains_out.start()
    for copy in w6:
        copy.wait_recv()
    for copy in (own_half, gains_out, row_out):
        copy.wait()
    for copy in [*zgather.values(), *pair, *xgather.values(), *xreduce.values(), *zreduce, dcopy, *w1.values(), gcopy, *g1, *g2, *g3, *w5.values(), *g5, *w6]:
        copy.wait_send()
    for r in range(3):
        pl.when(zl != r)(lambda r=r: second(r).wait_send())

    def sent():
        for d in range(1, 4):
            across(d).wait_send()
            fourth(d, 0).wait_send()

    pl.when(zl < 3)(sent)


def widen(grad_ref, row_ref, gain_ref, row_out, wide_ref, gain_out, grad, wide, row, gain, rowv, gainv, in_sem, out_sem):
    quarter = D // 4
    at = [pl.ds(q * quarter, quarter) for q in range(4)]
    reads = [pltpu.make_async_copy(grad_ref.at[at[q], :], grad.at[at[q], :], in_sem.at[q]) for q in range(4)]
    reads += [pltpu.make_async_copy(row_ref, rowv, in_sem.at[4]), pltpu.make_async_copy(gain_ref, gainv, in_sem.at[5])]
    for copy in reads:
        copy.start()
    writes = []
    for q in range(4):
        reads[q].wait()
        wide[at[q], :] = grad[at[q], :].astype(F32)
        writes.append(pltpu.make_async_copy(wide.at[at[q], :], wide_ref.at[at[q], :], out_sem.at[q]))
        writes[-1].start()
    reads[4].wait()
    reads[5].wait()
    for b in range(BLOCKS):
        cols = slice(b * LANE, (b + 1) * LANE)
        row[:, cols] = rowv[b : b + 1, :]
        gain[0:1, cols] = gainv[b]
        gain[1:2, cols] = gainv[BLOCKS + b]
    writes += [pltpu.make_async_copy(row, row_out, out_sem.at[4]), pltpu.make_async_copy(gain, gain_out, out_sem.at[5])]
    for copy in writes[4:]:
        copy.start()
    for copy in writes:
        copy.wait()


def shards(tokens, norm_gains, enc_weight, head_weight, head_bias, positives):
    vmem, dma = pltpu.VMEM, pltpu.SemaphoreType.DMA
    anywhere = pl.BlockSpec(memory_space=pl.ANY)
    scratch = [
        vmem((1, SEQ, D), BF16),
        vmem((2, D), F32),
        vmem((D, D), BF16),
        vmem((1, 8), jnp.int32),
        vmem((2, SHARD, D), BF16),
        vmem((SHARD,), BF16),
        vmem((SHARD,), BF16),
        vmem((SEQ, D), BF16),
        vmem((2, 2, SEQ, HALF), BF16),
        vmem((SEQ, D), BF16),
        vmem((2, SEQ, HALF), BF16),
        vmem((D, HALF), F32),
        vmem((D, HALF), F32),
        vmem((D, D), F32),
        vmem((SEQ, D), F32),
        vmem((8, LANE), F32),
        vmem((8, LANE), F32),
        vmem((8, LANE), F32),
        vmem((NZ, 8, LANE), BF16),
        vmem((NZ * 8, LANE), F32),
        vmem((NP, 2, 8, D + LANE), BF16),
        vmem((NP, 2, 8, D), BF16),
        vmem((NP, 2, 8, D), BF16),
        vmem((2, 8, D), F32),
        vmem((NZ * 8, LANE), F32),
        vmem((NZ * 8, LANE), F32),
        vmem((8, LANE), F32),
        vmem((8, LANE), F32),
        vmem((NP, 3, 16, HALF), BF16),
        vmem((NP, 3, 16, HALF), BF16),
        vmem((3, 16, HALF), F32),
        vmem((NP, 1, LANE), F32),
        vmem((NP, 1, LANE), F32),
        vmem((NP, 1, LANE), F32),
        vmem((3, 16, HALF), F32),
        vmem((4, 16, HALF), F32),
        vmem((4, 16, HALF), F32),
        vmem((8, 1, LANE), F32),
        vmem((NP, 1, LANE), F32),
        vmem((NP, 1, LANE), F32),
        vmem((D, HALF), BF16),
        vmem((8, LANE), F32),
        dma((6,)),
        dma((6,)), dma((6,)),
        dma((NZ,)), dma((NZ,)),
        dma((2 * NP,)), dma((2 * NP,)),
        dma((2 * NP,)), dma((2 * NP,)),
        dma((NZ,)), dma((NZ,)),
        dma((3 * NP,)), dma((3 * NP,)),
        dma((NP,)), dma((NP,)),
        dma((4,)), dma((4,)),
        dma((4,)), dma((4,)),
        dma((4,)), dma((4,)),
        dma((4,)), dma((4,)),
        dma((4,)), dma((4,)),
        dma((3 * NP,)), dma((3 * NP,)),
        dma((NP,)), dma((NP,)),
        dma((3 * NP,)), dma((3 * NP,)),
    ]
    row_part, grad, gain_part = pl.pallas_call(
        kernel,
        out_shape=(
            jax.ShapeDtypeStruct((8, LANE), F32),
            jax.ShapeDtypeStruct((D, D), BF16),
            jax.ShapeDtypeStruct((NP, 1, LANE), F32),
        ),
        in_specs=[anywhere] * 6,
        out_specs=(anywhere,) * 3,
        scratch_shapes=scratch,
        compiler_params=pltpu.CompilerParams(collective_id=0, has_side_effects=True),
    )(tokens, norm_gains, enc_weight, head_weight, head_bias, positives)
    return pl.pallas_call(
        widen,
        out_shape=tuple(jax.ShapeDtypeStruct((rows, D), F32) for rows in (1, D, 2)),
        in_specs=[anywhere] * 3,
        out_specs=(anywhere,) * 3,
        scratch_shapes=[
            vmem((D, D), BF16), vmem((D, D), F32), vmem((1, D), F32), vmem((2, D), F32),
            vmem((8, LANE), F32), vmem((NP, 1, LANE), F32), dma((6,)), dma((6,)),
        ],
    )(grad, row_part, gain_part)


def solution(mesh):
    placed = (P(("label", "doc"), None, None), P(), P(), P(("label", "doc"), None), P(("label", "doc")), P(("label", "doc"), None))
    return jax.shard_map(
        shards, mesh=mesh, in_specs=placed, out_specs=(P(("label", "doc"), None), P(), P()), check_vma=False
    )
```

```python
import math

import jax
import jax.numpy as jnp
from jax import lax
from jax.experimental import pallas as pl
from jax.experimental.pallas import tpu as pltpu
from jax.sharding import PartitionSpec as P

D, SEQ, SHARD = 768, 128, 512
NZ, NX, NY, NP = 16, 4, 4, 16
LANE, HALF, ROWS = 128, 384, 48
BLOCKS = D // LANE
EPSILON = 1e-05
BF16, F32 = jnp.bfloat16, jnp.float32
MESH = pl.DeviceIdType.MESH
ROOT = math.sqrt(2.0 / math.pi)
STEP = (0, 1, 2, 3, 4, 13, 14, 15, 5, 6, 7, 8, 9, 10, 11, 12)
FAR_FIRST = (11, 10, 12, 9, 13, 8, 14, 15, 4, 3, 5, 2, 6, 1, 7)
WITHIN_4 = (15, 4, 5, 3, 6, 2, 7, 1)
RELAYS = ((1, 4, 8, 4), (5, 3, 12, 12))
PAIRS = ((0, 1), (3, 2))
PLANE = tuple(4 * dx + dy for pair in PAIRS for dx in pair for dy in (1, 3, 2, 0) if dx or dy)


def device(z, x, y, c):
    return (z * 4 + lax.div(x, 2) * 2 + c, y * 2 + lax.rem(x, 2))


def contract(a, b, dims):
    return lax.dot_general(a, b, ((dims[:1], dims[1:]), ((), ())), preferred_element_type=F32)


def high_low(v):
    high = v.astype(BF16)
    return high, (v - high.astype(F32)).astype(BF16)


def kernel(
    tok_hbm, gains_hbm, enc_hbm, head_hbm, bias_hbm, pos_hbm,
    row_ref, grad_ref, gain_ref,
    tok_ref, gains_ref, enc_ref, pos_ref, head, bias0, bias1, act, gel, act2, gel2, bo, bp, pm, nrm, r8, g8, zs, zbuf, zf, xbuf,
    rs, rr, rown, rz, rzr, dpo, dpp, ws, wr, wown, gs1, gs1p, gr1, s2, s2r, s3r, g2r, g3r, gfin, half, rowout,
    local_sem, pair_send, pair_recv, za_s, za_r, xa_s, xa_r, xr_s, xr_r, zr_s, zr_r,
    w1_s, w1_r, g1_s, g1_r, w2_s, w2_r, g2_s, g2_r, w3_s, w3_r, g3_s, g3_r,
    w4_s, w4_r, w5_s, w5_r, g5_s, g5_r, w6_s, w6_r,
):
    label, doc = lax.axis_index("label"), lax.axis_index("doc")
    z, c = lax.div(label, 4), lax.rem(label, 2)
    x, y = lax.rem(lax.div(label, 2), 2) * 2 + lax.rem(doc, 2), lax.div(doc, 2)
    zh, zl = lax.div(z, 4), lax.rem(z, 4)
    me = x * 4 + y
    partner = device(z, x, y, 1 - c)

    def along(k):
        return device(lax.rem(z + k, NZ), x, y, c)

    def shifted(i):
        return lax.rem(x + i // 4, NX), lax.rem(y + i % 4, NY)

    def plane(i):
        return device(z, *shifted(i), c)

    def back(i):
        return (4 - i // 4) % 4 * 4 + (4 - i % 4) % 4

    def send(src, dst, send_sem, recv_sem, to):
        copy = pltpu.make_async_remote_copy(
            src_ref=src, dst_ref=dst, send_sem=send_sem, recv_sem=recv_sem, device_id=to, device_id_type=MESH
        )
        copy.start()
        return copy

    local = [
        pltpu.make_async_copy(src, dst, local_sem.at[n])
        for n, (src, dst) in enumerate((
            (tok_hbm, tok_ref), (gains_hbm, gains_ref), (enc_hbm, enc_ref), (pos_hbm, pos_ref),
            (head_hbm, head.at[0]), (bias_hbm, bias0),
        ))
    ]
    for copy in local[:4]:
        copy.start()
    barrier = pltpu.get_barrier_semaphore()
    for to in [partner] + [along(STEP[k]) for k in WITHIN_4] + [plane(i) for i in PLANE]:
        pl.semaphore_signal(barrier, inc=1, device_id=to, device_id_type=MESH)

    for copy in local[4:]:
        copy.start()

    local[0].wait()
    local[1].wait()
    tok = tok_ref[0].astype(F32)
    center = tok - jnp.mean(tok, axis=-1, keepdims=True)
    normed = center * lax.rsqrt(jnp.mean(center * center, axis=-1, keepdims=True) + EPSILON)
    nrm[...] = normed
    act[...] = (normed * gains_ref[0:1, :]).astype(BF16)
    local[2].wait()
    pre = jnp.dot(act[...], enc_ref[...], preferred_element_type=F32)
    tanh = jnp.tanh(ROOT * (pre + 0.044715 * (pre * pre * pre)))
    cdf = 0.5 * (1.0 + tanh)
    pooled = jnp.mean(tok + pre * cdf, axis=0, keepdims=True)
    for b in range(BLOCKS):
        r8[b : b + 1, :] = pooled[:, b * LANE : (b + 1) * LANE]
        g8[b : b + 1, :] = gains_ref[1:2, b * LANE : (b + 1) * LANE]
    pooled = r8[0:BLOCKS, :]
    gain = g8[0:BLOCKS, :]
    center = pooled - jnp.sum(pooled) / D
    inverse = lax.rsqrt(jnp.sum(center * center, keepdims=True) / D + EPSILON)
    normed_out = center * inverse
    zs[...] = jnp.zeros_like(zs)
    zs[0:BLOCKS, :] = normed_out * gain
    local[3].wait()
    ids = pos_ref[...]
    zs[6:7, 0:8] = (jnp.where(ids < 0, 512, jnp.right_shift(ids, 9)) - 256).astype(F32)
    zs[7:8, 0:8] = (jnp.bitwise_and(ids, 511) - 256).astype(F32)
    zbuf[0] = zs[...].astype(BF16)

    pl.semaphore_wait(barrier, 24)
    zgather = {k: send(zbuf.at[0], zbuf.at[k], za_s.at[k], za_r.at[k], along(STEP[k])) for k in WITHIN_4}
    pair = [
        send(head_hbm, head.at[1], pair_send.at[0], pair_recv.at[0], partner),
        send(bias_hbm, bias1, pair_send.at[1], pair_recv.at[1], partner),
    ]

    slope = cdf + (0.5 * ROOT) * pre * (1.0 - tanh * tanh) * (1.0 + 0.134145 * (pre * pre))
    high, low = high_low(slope)
    for h in range(2):
        gel[h, 0] = high[:, h * HALF : (h + 1) * HALF]
        gel[h, 1] = low[:, h * HALF : (h + 1) * HALF]
    pair += [
        send(act, act2, pair_send.at[2], pair_recv.at[2], partner),
        send(gel.at[1 - c], gel2, pair_send.at[3], pair_recv.at[3], partner),
    ]
    for q in range(3):
        cols = slice(q * 256, (q + 1) * 256)
        n_high, n_low = high_low(nrm[:, cols])
        for h in range(2):
            block = contract(n_high, gel[h, 0], (0, 0)) + contract(n_low, gel[h, 0], (0, 0)) + contract(n_high, gel[h, 1], (0, 0))
            pm[cols, h * HALF : (h + 1) * HALF] = block * enc_ref[cols, h * HALF : (h + 1) * HALF].astype(F32)
    for ref in (rz, dpo, gs1):
        ref[...] = jnp.zeros_like(ref)

    relays = []
    for n, (first, count, slot, step) in enumerate(RELAYS):
        for k in range(first, first + count):
            zgather[k].wait_recv()
        relays.append(
            send(zbuf.at[pl.ds(first, count)], zbuf.at[pl.ds(slot, count)], za_s.at[8 + n], za_r.at[8 + n], along(step))
        )
    xgather = {}
    for h in range(2):
        if h:
            for copy in [zgather[15], *relays]:
                copy.wait_recv()
        zf[64 * h : 64 * h + 64, :] = zbuf[8 * h : 8 * h + 8].reshape(64, LANE).astype(F32)
        for b in range(BLOCKS):
            xbuf[0, h, :, b * LANE : (b + 1) * LANE] = zf[pl.ds(64 * h + b, 8, stride=8), :].astype(BF16)
        first, second = zf[pl.ds(64 * h + 6, 8, stride=8), :], zf[pl.ds(64 * h + 7, 8, stride=8), :]
        lanes = lax.broadcasted_iota(jnp.int32, (8, LANE), 1)
        xbuf[0, h, :, D:] = jnp.where(lanes < 8, first, pltpu.roll(second, 8, 1)).astype(BF16)
        for i in PLANE:
            at = 2 * i + h
            xgather[i, h] = send(xbuf.at[0, h], xbuf.at[i, h], xa_s.at[at], xa_r.at[at], plane(i))

    for copy in pair[2:]:
        copy.wait_recv()
    for q in range(3):
        cols = slice(q * 256, (q + 1) * 256)
        bo[cols, :] = contract(act[:, cols], gel[c, 0], (0, 0)) + contract(act[:, cols], gel[c, 1], (0, 0))
        bp[cols, :] = contract(act2[:, cols], gel2[0], (0, 0)) + contract(act2[:, cols], gel2[1], (0, 0))
    local[4].wait()
    local[5].wait()
    for copy in pair[:2]:
        copy.wait_recv()

    flat = label * 8 + doc
    bases = (flat * SHARD, (flat + (1 - 2 * c) * 8) * SHARD)
    spots = lax.broadcasted_iota(jnp.int32, (64, SHARD), 1)
    xreduce = {}
    for h, columns in [(h, columns) for h in range(2) for columns in PAIRS]:
        slots = [4 * dx + dy for dx in columns for dy in range(4)]
        for i in slots:
            if i:
                xgather[i, h].wait_recv()
        block = jnp.concatenate([xbuf[4 * dx : 4 * dx + 4, h].reshape(32, D + LANE) for dx in columns], axis=0)
        embed = block[:, 0:D]
        code = block[:, D:].astype(F32)
        ids = ((code + 256.0) * 512.0 + (pltpu.roll(code, LANE - 8, 1) + 256.0)).astype(jnp.int32)
        total = jnp.zeros((64, D), F32)
        for s in range(2):
            logits = contract(embed, head[s], (1, 1)) + (bias0, bias1)[s][...].astype(F32).reshape(1, SHARD)
            near = ids - bases[s]
            target = near[:, 0:1] == spots
            for q in range(1, 8):
                target = jnp.logical_or(target, near[:, q : q + 1] == spots)
            d_logit = (jax.nn.sigmoid(logits) - target.astype(F32)).astype(BF16)
            total += jnp.dot(d_logit, head[s], preferred_element_type=F32)
        for m, i in enumerate(slots):
            part = total[8 * m : 8 * m + 8]
            if i:
                rs[i, h] = part.astype(BF16)
            else:
                rown[h] = part
        for i in slots:
            if i:
                at = 2 * i + h
                xreduce[i, h] = send(rs.at[i, h], rr.at[i, h], xr_s.at[at], xr_r.at[at], plane(back(i)))
    zreduce = []
    for h in range(2):
        for i in PLANE:
            xreduce[i, h].wait_recv()
        total = rown[h]
        for i in range(1, NP):
            total += rr[i, h].astype(F32)
        for b in range(BLOCKS):
            rz[pl.ds(64 * h + b, 8, stride=8), :] = total[:, b * LANE : (b + 1) * LANE]
        for k in FAR_FIRST:
            if k // 8 == h:
                at = pl.ds(8 * k, 8)
                zreduce.append(send(rz.at[at, :], rzr.at[at, :], zr_s.at[k], zr_r.at[k], along(NZ - STEP[k])))
    for copy in zreduce:
        copy.wait_recv()
    rowg = rz[0:8, :]
    for k in range(1, NZ):
        rowg += rzr[8 * k : 8 * k + 8, :]

    cot = rowg[0:BLOCKS]
    d_normed = cot * gain
    d_pooled = inverse * (d_normed - jnp.sum(d_normed) / D - normed_out * (jnp.sum(d_normed * normed_out) / D))
    dpo[0:BLOCKS, :] = d_pooled / SEQ
    dcopy = send(dpo, dpp, pair_send.at[4], pair_recv.at[4], partner)
    rowout[...] = rowg
    row_out = pltpu.make_async_copy(rowout, row_ref, local_sem.at[2])
    row_out.start()
    dcopy.wait_recv()
    mine = jnp.concatenate([dpo[pl.ds(3 * c + b, 1), :] for b in range(3)], axis=1)
    theirs = jnp.concatenate([dpp[pl.ds(3 * c + b, 1), :] for b in range(3)], axis=1)

    def weight_block(spot, r):
        at = pl.ds(pl.multiple_of(spot * ROWS + 16 * r, 16), 16)
        return bo[at, :] * mine + bp[at, :] * theirs

    w1 = {}
    for r in range(3):
        for i in PLANE:
            px, py = shifted(i)
            ws[i, r] = weight_block(px * 4 + py, r).astype(BF16)
        for i in PLANE:
            w1[i, r] = send(ws.at[i, r], wr.at[i, r], w1_s.at[3 * i + r], w1_r.at[3 * i + r], plane(i))
    for r in range(3):
        wown[r] = weight_block(me, r)
    lane_sum = pm[:, 0:LANE] * dpo[0:1, :]
    for b in range(1, BLOCKS):
        lane_sum += pm[:, b * LANE : (b + 1) * LANE] * dpo[b : b + 1, :]
    gain_in = lax.dot_general(
        jnp.ones((8, LANE), F32), lane_sum, (((1,), (1,)), ((), ())),
        precision=lax.Precision.HIGHEST, preferred_element_type=F32,
    )
    gain_out = cot * normed_out
    for b in range(BLOCKS):
        gs1[b] = gain_in[0:1, b * LANE : (b + 1) * LANE]
        gs1[BLOCKS + b] = gain_out[b : b + 1, :]
    gcopy = send(gs1, gs1p, pair_send.at[5], pair_recv.at[5], partner)
    gcopy.wait_recv()
    g3r[...] = gs1[...] + gs1p[...]
    g1 = []
    for i in PLANE:
        px, py = shifted(i)
        g1.append(send(g3r.at[px * 4 + py], gr1.at[i], g1_s.at[i], g1_r.at[i], plane(i)))

    near_z = [lax.rem(zl + d, 4) for d in range(4)]

    def cube(d):
        return device(zh * 4 + near_z[d], x, y, c)

    def cubes(d):
        return along(4 * d)

    def piece(spot, r):
        return half.at[pl.ds(pl.multiple_of(spot * ROWS + 16 * r, 16), 16), :]

    def placed(spot, r):
        rows = pl.ds(pl.multiple_of(spot * ROWS + 16 * r, 16), 16)
        return grad_ref.at[rows, pl.ds(pl.multiple_of(c * HALF, LANE), HALF)]

    def second(r):
        d = lax.rem(r + 4 - zl, 4)
        return pltpu.make_async_remote_copy(
            src_ref=s2.at[r], dst_ref=s2r.at[d], send_sem=w2_s.at[r], recv_sem=w2_r.at[d],
            device_id=device(zh * 4 + r, x, y, c), device_id_type=MESH,
        )

    def landed(d):
        return pltpu.make_async_remote_copy(
            src_ref=s2r.at[d], dst_ref=s2r.at[d], send_sem=w2_s.at[0], recv_sem=w2_r.at[d],
            device_id=cube(d), device_id_type=MESH,
        )

    def across(d):
        return pltpu.make_async_remote_copy(
            src_ref=s3r.at[zh], dst_ref=s3r.at[zh], send_sem=w3_s.at[d], recv_sem=w3_r.at[d],
            device_id=cubes(d), device_id_type=MESH,
        )

    def fourth(d, r):
        return pltpu.make_async_remote_copy(
            src_ref=piece(me, r), dst_ref=piece(me, r), send_sem=w4_s.at[d], recv_sem=w4_r.at[r],
            device_id=cube(d), device_id_type=MESH,
        )

    def start_across(r):
        for d in range(1, 4):
            landed(d).wait_recv()
        s3r[zh] = s2[r] + s2r[1] + s2r[2] + s2r[3]
        for d in range(1, 4):
            across(d).start()

    def end_across(r):
        for d in range(1, 4):
            across(d).wait_recv()
        whole = s3r[0] + s3r[1] + s3r[2] + s3r[3]
        piece(me, r)[...] = whole.astype(BF16)
        for d in range(1, 4):
            fourth(d, r).start()

    for r in range(3):
        for i in PLANE:
            w1[i, r].wait_recv()
        total = wown[r]
        for i in range(1, NP):
            total += wr[i, r].astype(F32)
        s2[r] = total
        pl.when(zl != r)(lambda r=r: second(r).start())
        if r == 1:
            pl.when(zl == 0)(lambda: start_across(0))
    pl.when(zl == 1)(lambda: start_across(1))
    pl.when(zl == 2)(lambda: start_across(2))
    for copy in g1:
        copy.wait_recv()
    gsum = g3r[me]
    for i in range(1, NP):
        gsum += gr1[i]
    g2r[zl] = gsum
    g2 = [send(g2r.at[zl], g2r.at[zl], g2_s.at[d], g2_r.at[d], cube(d)) for d in range(1, 4)]
    for copy in g2:
        copy.wait_recv()
    g2r[4 + zh] = g2r[0] + g2r[1] + g2r[2] + g2r[3]
    g3 = [send(g2r.at[4 + zh], g2r.at[4 + zh], g3_s.at[d], g3_r.at[d], cubes(d)) for d in range(1, 4)]

    w5, w6 = {}, []
    for r in range(3):
        if r == 2:
            for copy in g3:
                copy.wait_recv()
            gfin[me] = g2r[4] + g2r[5] + g2r[6] + g2r[7]
            g5 = [send(gfin.at[me], gfin.at[me], g5_s.at[i], g5_r.at[i], plane(i)) for i in PLANE]
        pl.when(zl == r)(lambda r=r: end_across(r))
        pl.when(zl != r)(lambda r=r: fourth(1, r).wait_recv())
        for i in PLANE:
            w5[i, r] = send(piece(me, r), piece(me, r), w5_s.at[3 * i + r], w5_r.at[3 * i + r], plane(i))
        w6.append(send(piece(me, r), placed(me, r), w6_s.at[r], w6_r.at[r], partner))
    for r in range(3):
        for i in PLANE:
            w5[i, r].wait_recv()
            px, py = shifted(back(i))
            spot = px * 4 + py
            w6.append(send(piece(spot, r), placed(spot, r), w6_s.at[3 * i + r], w6_r.at[3 * i + r], partner))
    own_half = pltpu.make_async_copy(half, grad_ref.at[:, pl.ds(pl.multiple_of(c * HALF, LANE), HALF)], local_sem.at[0])
    own_half.start()
    for copy in g5:
        copy.wait_recv()
    gains_out = pltpu.make_async_copy(gfin, gain_ref, local_sem.at[1])
    gains_out.start()
    for copy in w6:
        copy.wait_recv()
    for copy in (own_half, gains_out, row_out):
        copy.wait()
    for copy in [*zgather.values(), *relays, *pair, *xgather.values(), *xreduce.values(), *zreduce, dcopy, *w1.values(), gcopy, *g1, *g2, *g3, *w5.values(), *g5, *w6]:
        copy.wait_send()
    for r in range(3):
        pl.when(zl != r)(lambda r=r: second(r).wait_send())

    def sent():
        for d in range(1, 4):
            across(d).wait_send()
            fourth(d, 0).wait_send()

    pl.when(zl < 3)(sent)


def widen(grad_ref, row_ref, gain_ref, row_out, wide_ref, gain_out, grad, wide, row, gain, rowv, gainv, in_sem, out_sem):
    quarter = D // 4
    at = [pl.ds(q * quarter, quarter) for q in range(4)]
    reads = [pltpu.make_async_copy(grad_ref.at[at[q], :], grad.at[at[q], :], in_sem.at[q]) for q in range(4)]
    reads += [pltpu.make_async_copy(row_ref, rowv, in_sem.at[4]), pltpu.make_async_copy(gain_ref, gainv, in_sem.at[5])]
    for copy in reads:
        copy.start()
    writes = []
    for q in range(4):
        reads[q].wait()
        wide[at[q], :] = grad[at[q], :].astype(F32)
        writes.append(pltpu.make_async_copy(wide.at[at[q], :], wide_ref.at[at[q], :], out_sem.at[q]))
        writes[-1].start()
    reads[4].wait()
    reads[5].wait()
    for b in range(BLOCKS):
        cols = slice(b * LANE, (b + 1) * LANE)
        row[:, cols] = rowv[b : b + 1, :]
        gain[0:1, cols] = gainv[b]
        gain[1:2, cols] = gainv[BLOCKS + b]
    writes += [pltpu.make_async_copy(row, row_out, out_sem.at[4]), pltpu.make_async_copy(gain, gain_out, out_sem.at[5])]
    for copy in writes[4:]:
        copy.start()
    for copy in writes:
        copy.wait()


def shards(tokens, norm_gains, enc_weight, head_weight, head_bias, positives):
    vmem, dma = pltpu.VMEM, pltpu.SemaphoreType.DMA
    anywhere = pl.BlockSpec(memory_space=pl.ANY)
    scratch = [
        vmem((1, SEQ, D), BF16),
        vmem((2, D), F32),
        vmem((D, D), BF16),
        vmem((1, 8), jnp.int32),
        vmem((2, SHARD, D), BF16),
        vmem((SHARD,), BF16),
        vmem((SHARD,), BF16),
        vmem((SEQ, D), BF16),
        vmem((2, 2, SEQ, HALF), BF16),
        vmem((SEQ, D), BF16),
        vmem((2, SEQ, HALF), BF16),
        vmem((D, HALF), F32),
        vmem((D, HALF), F32),
        vmem((D, D), F32),
        vmem((SEQ, D), F32),
        vmem((8, LANE), F32),
        vmem((8, LANE), F32),
        vmem((8, LANE), F32),
        vmem((NZ, 8, LANE), BF16),
        vmem((NZ * 8, LANE), F32),
        vmem((NP, 2, 8, D + LANE), BF16),
        vmem((NP, 2, 8, D), BF16),
        vmem((NP, 2, 8, D), BF16),
        vmem((2, 8, D), F32),
        vmem((NZ * 8, LANE), F32),
        vmem((NZ * 8, LANE), F32),
        vmem((8, LANE), F32),
        vmem((8, LANE), F32),
        vmem((NP, 3, 16, HALF), BF16),
        vmem((NP, 3, 16, HALF), BF16),
        vmem((3, 16, HALF), F32),
        vmem((NP, 1, LANE), F32),
        vmem((NP, 1, LANE), F32),
        vmem((NP, 1, LANE), F32),
        vmem((3, 16, HALF), F32),
        vmem((4, 16, HALF), F32),
        vmem((4, 16, HALF), F32),
        vmem((8, 1, LANE), F32),
        vmem((NP, 1, LANE), F32),
        vmem((NP, 1, LANE), F32),
        vmem((D, HALF), BF16),
        vmem((8, LANE), F32),
        dma((6,)),
        dma((6,)), dma((6,)),
        dma((NZ,)), dma((NZ,)),
        dma((2 * NP,)), dma((2 * NP,)),
        dma((2 * NP,)), dma((2 * NP,)),
        dma((NZ,)), dma((NZ,)),
        dma((3 * NP,)), dma((3 * NP,)),
        dma((NP,)), dma((NP,)),
        dma((4,)), dma((4,)),
        dma((4,)), dma((4,)),
        dma((4,)), dma((4,)),
        dma((4,)), dma((4,)),
        dma((4,)), dma((4,)),
        dma((3 * NP,)), dma((3 * NP,)),
        dma((NP,)), dma((NP,)),
        dma((3 * NP,)), dma((3 * NP,)),
    ]
    row_part, grad, gain_part = pl.pallas_call(
        kernel,
        out_shape=(
            jax.ShapeDtypeStruct((8, LANE), F32),
            jax.ShapeDtypeStruct((D, D), BF16),
            jax.ShapeDtypeStruct((NP, 1, LANE), F32),
        ),
        in_specs=[anywhere] * 6,
        out_specs=(anywhere,) * 3,
        scratch_shapes=scratch,
        compiler_params=pltpu.CompilerParams(collective_id=0, has_side_effects=True),
    )(tokens, norm_gains, enc_weight, head_weight, head_bias, positives)
    return pl.pallas_call(
        widen,
        out_shape=tuple(jax.ShapeDtypeStruct((rows, D), F32) for rows in (1, D, 2)),
        in_specs=[anywhere] * 3,
        out_specs=(anywhere,) * 3,
        scratch_shapes=[
            vmem((D, D), BF16), vmem((D, D), F32), vmem((1, D), F32), vmem((2, D), F32),
            vmem((8, LANE), F32), vmem((NP, 1, LANE), F32), dma((6,)), dma((6,)),
        ],
    )(grad, row_part, gain_part)


def solution(mesh):
    placed = (P(("label", "doc"), None, None), P(), P(), P(("label", "doc"), None), P(("label", "doc")), P(("label", "doc"), None))
    return jax.shard_map(
        shards, mesh=mesh, in_specs=placed, out_specs=(P(("label", "doc"), None), P(), P()), check_vma=False
    )
```

```python
import math

import jax
import jax.numpy as jnp
from jax import lax
from jax.experimental import pallas as pl
from jax.experimental.pallas import tpu as pltpu
from jax.sharding import PartitionSpec as P

D, SEQ, SHARD = 768, 128, 512
NZ, NX, NY, NP = 16, 4, 4, 16
LANE, HALF, ROWS = 128, 384, 48
BLOCKS = D // LANE
EPSILON = 1e-05
BF16, F32 = jnp.bfloat16, jnp.float32
MESH = pl.DeviceIdType.MESH
ROOT = math.sqrt(2.0 / math.pi)
STEP = (0, 1, 2, 3, 4, 13, 14, 15, 5, 6, 7, 8, 9, 10, 11, 12)
FAR_FIRST = (11, 10, 12, 9, 13, 8, 14, 15, 4, 3, 5, 2, 6, 1, 7)
SPREAD = (1, 4, 12, 3, 5, 13, 8, 2, 7, 15, 9, 6, 14, 11, 10)
WITHIN_4 = (15, 4, 5, 3, 6, 2, 7, 1)
RELAYS = ((1, 4, 8, 4), (5, 3, 12, 12))
PAIRS = ((0, 1), (3, 2))
PLANE = tuple(4 * dx + dy for pair in PAIRS for dx in pair for dy in (1, 3, 2, 0) if dx or dy)


def device(z, x, y, c):
    return (z * 4 + lax.div(x, 2) * 2 + c, y * 2 + lax.rem(x, 2))


def contract(a, b, dims):
    return lax.dot_general(a, b, ((dims[:1], dims[1:]), ((), ())), preferred_element_type=F32)


def high_low(v):
    high = v.astype(BF16)
    return high, (v - high.astype(F32)).astype(BF16)


def kernel(
    tok_hbm, gains_hbm, enc_hbm, head_hbm, bias_hbm, pos_hbm,
    row_ref, grad_ref, gain_ref,
    tok_ref, gains_ref, enc_ref, pos_ref, head, bias0, bias1, act, gel, act2, gel2, bo, bp, pm, nrm, r8, g8, zs, zbuf, zf, xbuf,
    rs, rr, rown, rz, rzr, dpo, dpp, ws, wr, wown, gs1, gs1p, gr1, s2, s2r, s3r, g2r, g3r, gfin, half, rowout,
    local_sem, pair_send, pair_recv, za_s, za_r, xa_s, xa_r, xr_s, xr_r, zr_s, zr_r,
    w1_s, w1_r, g1_s, g1_r, w2_s, w2_r, g2_s, g2_r, w3_s, w3_r, g3_s, g3_r,
    w4_s, w4_r, w5_s, w5_r, g5_s, g5_r, w6_s, w6_r,
):
    label, doc = lax.axis_index("label"), lax.axis_index("doc")
    z, c = lax.div(label, 4), lax.rem(label, 2)
    x, y = lax.rem(lax.div(label, 2), 2) * 2 + lax.rem(doc, 2), lax.div(doc, 2)
    zh, zl = lax.div(z, 4), lax.rem(z, 4)
    me = x * 4 + y
    partner = device(z, x, y, 1 - c)

    def along(k):
        return device(lax.rem(z + k, NZ), x, y, c)

    def shifted(i):
        return lax.rem(x + i // 4, NX), lax.rem(y + i % 4, NY)

    def plane(i):
        return device(z, *shifted(i), c)

    def back(i):
        return (4 - i // 4) % 4 * 4 + (4 - i % 4) % 4

    def send(src, dst, send_sem, recv_sem, to):
        copy = pltpu.make_async_remote_copy(
            src_ref=src, dst_ref=dst, send_sem=send_sem, recv_sem=recv_sem, device_id=to, device_id_type=MESH
        )
        copy.start()
        return copy

    local = [
        pltpu.make_async_copy(src, dst, local_sem.at[n])
        for n, (src, dst) in enumerate((
            (tok_hbm, tok_ref), (gains_hbm, gains_ref), (enc_hbm, enc_ref), (pos_hbm, pos_ref),
            (head_hbm, head.at[0]), (bias_hbm, bias0),
        ))
    ]
    for copy in local[:4]:
        copy.start()
    barrier = pltpu.get_barrier_semaphore()
    for to in [partner] + [along(STEP[k]) for k in WITHIN_4] + [plane(i) for i in PLANE]:
        pl.semaphore_signal(barrier, inc=1, device_id=to, device_id_type=MESH)

    for copy in local[4:]:
        copy.start()

    local[0].wait()
    local[1].wait()
    tok = tok_ref[0].astype(F32)
    center = tok - jnp.mean(tok, axis=-1, keepdims=True)
    normed = center * lax.rsqrt(jnp.mean(center * center, axis=-1, keepdims=True) + EPSILON)
    nrm[...] = normed
    act[...] = (normed * gains_ref[0:1, :]).astype(BF16)
    local[2].wait()
    pre = jnp.dot(act[...], enc_ref[...], preferred_element_type=F32)
    tanh = jnp.tanh(ROOT * (pre + 0.044715 * (pre * pre * pre)))
    cdf = 0.5 * (1.0 + tanh)
    pooled = jnp.mean(tok + pre * cdf, axis=0, keepdims=True)
    for b in range(BLOCKS):
        r8[b : b + 1, :] = pooled[:, b * LANE : (b + 1) * LANE]
        g8[b : b + 1, :] = gains_ref[1:2, b * LANE : (b + 1) * LANE]
    pooled = r8[0:BLOCKS, :]
    gain = g8[0:BLOCKS, :]
    center = pooled - jnp.sum(pooled) / D
    inverse = lax.rsqrt(jnp.sum(center * center, keepdims=True) / D + EPSILON)
    normed_out = center * inverse
    zs[...] = jnp.zeros_like(zs)
    zs[0:BLOCKS, :] = normed_out * gain
    local[3].wait()
    ids = pos_ref[...]
    zs[6:7, 0:8] = (jnp.where(ids < 0, 512, jnp.right_shift(ids, 9)) - 256).astype(F32)
    zs[7:8, 0:8] = (jnp.bitwise_and(ids, 511) - 256).astype(F32)
    zbuf[0] = zs[...].astype(BF16)

    pl.semaphore_wait(barrier, 24)
    zgather = {k: send(zbuf.at[0], zbuf.at[k], za_s.at[k], za_r.at[k], along(STEP[k])) for k in WITHIN_4}
    pair = [
        send(head_hbm, head.at[1], pair_send.at[0], pair_recv.at[0], partner),
        send(bias_hbm, bias1, pair_send.at[1], pair_recv.at[1], partner),
    ]

    slope = cdf + (0.5 * ROOT) * pre * (1.0 - tanh * tanh) * (1.0 + 0.134145 * (pre * pre))
    high, low = high_low(slope)
    for h in range(2):
        gel[h, 0] = high[:, h * HALF : (h + 1) * HALF]
        gel[h, 1] = low[:, h * HALF : (h + 1) * HALF]
    pair += [
        send(act, act2, pair_send.at[2], pair_recv.at[2], partner),
        send(gel.at[1 - c], gel2, pair_send.at[3], pair_recv.at[3], partner),
    ]
    for q in range(3):
        cols = slice(q * 256, (q + 1) * 256)
        n_high, n_low = high_low(nrm[:, cols])
        for h in range(2):
            block = contract(n_high, gel[h, 0], (0, 0)) + contract(n_low, gel[h, 0], (0, 0)) + contract(n_high, gel[h, 1], (0, 0))
            pm[cols, h * HALF : (h + 1) * HALF] = block * enc_ref[cols, h * HALF : (h + 1) * HALF].astype(F32)
    for ref in (rz, dpo, gs1):
        ref[...] = jnp.zeros_like(ref)

    relays = []
    for n, (first, count, slot, step) in enumerate(RELAYS):
        for k in range(first, first + count):
            zgather[k].wait_recv()
        relays.append(
            send(zbuf.at[pl.ds(first, count)], zbuf.at[pl.ds(slot, count)], za_s.at[8 + n], za_r.at[8 + n], along(step))
        )
    xgather = {}
    for h in range(2):
        if h:
            for copy in [zgather[15], *relays]:
                copy.wait_recv()
        zf[64 * h : 64 * h + 64, :] = zbuf[8 * h : 8 * h + 8].reshape(64, LANE).astype(F32)
        for b in range(BLOCKS):
            xbuf[0, h, :, b * LANE : (b + 1) * LANE] = zf[pl.ds(64 * h + b, 8, stride=8), :].astype(BF16)
        first, second = zf[pl.ds(64 * h + 6, 8, stride=8), :], zf[pl.ds(64 * h + 7, 8, stride=8), :]
        lanes = lax.broadcasted_iota(jnp.int32, (8, LANE), 1)
        xbuf[0, h, :, D:] = jnp.where(lanes < 8, first, pltpu.roll(second, 8, 1)).astype(BF16)
        for i in PLANE:
            at = 2 * i + h
            xgather[i, h] = send(xbuf.at[0, h], xbuf.at[i, h], xa_s.at[at], xa_r.at[at], plane(i))

    for copy in pair[2:]:
        copy.wait_recv()
    for q in range(3):
        cols = slice(q * 256, (q + 1) * 256)
        bo[cols, :] = contract(act[:, cols], gel[c, 0], (0, 0)) + contract(act[:, cols], gel[c, 1], (0, 0))
        bp[cols, :] = contract(act2[:, cols], gel2[0], (0, 0)) + contract(act2[:, cols], gel2[1], (0, 0))
    local[4].wait()
    local[5].wait()
    for copy in pair[:2]:
        copy.wait_recv()

    flat = label * 8 + doc
    bases = (flat * SHARD, (flat + (1 - 2 * c) * 8) * SHARD)
    spots = lax.broadcasted_iota(jnp.int32, (64, SHARD), 1)
    xreduce = {}
    for h, columns in [(h, columns) for h in range(2) for columns in PAIRS]:
        slots = [4 * dx + dy for dx in columns for dy in range(4)]
        for i in slots:
            if i:
                xgather[i, h].wait_recv()
        block = jnp.concatenate([xbuf[4 * dx : 4 * dx + 4, h].reshape(32, D + LANE) for dx in columns], axis=0)
        embed = block[:, 0:D]
        code = block[:, D:].astype(F32)
        ids = ((code + 256.0) * 512.0 + (pltpu.roll(code, LANE - 8, 1) + 256.0)).astype(jnp.int32)
        total = jnp.zeros((64, D), F32)
        for s in range(2):
            logits = contract(embed, head[s], (1, 1)) + (bias0, bias1)[s][...].astype(F32).reshape(1, SHARD)
            near = ids - bases[s]
            target = near[:, 0:1] == spots
            for q in range(1, 8):
                target = jnp.logical_or(target, near[:, q : q + 1] == spots)
            d_logit = (jax.nn.sigmoid(logits) - target.astype(F32)).astype(BF16)
            total += jnp.dot(d_logit, head[s], preferred_element_type=F32)
        for m, i in enumerate(slots):
            part = total[8 * m : 8 * m + 8]
            if i:
                rs[i, h] = part.astype(BF16)
            else:
                rown[h] = part
        for i in slots:
            if i:
                at = 2 * i + h
                xreduce[i, h] = send(rs.at[i, h], rr.at[i, h], xr_s.at[at], xr_r.at[at], plane(back(i)))
    zreduce = []
    for h in range(2):
        for i in PLANE:
            xreduce[i, h].wait_recv()
        total = rown[h]
        for i in range(1, NP):
            total += rr[i, h].astype(F32)
        for b in range(BLOCKS):
            rz[pl.ds(64 * h + b, 8, stride=8), :] = total[:, b * LANE : (b + 1) * LANE]
        for k in FAR_FIRST:
            if k // 8 == h:
                at = pl.ds(8 * k, 8)
                zreduce.append(send(rz.at[at, :], rzr.at[at, :], zr_s.at[k], zr_r.at[k], along(NZ - STEP[k])))
    for copy in zreduce:
        copy.wait_recv()
    rowg = rz[0:8, :]
    for k in range(1, NZ):
        rowg += rzr[8 * k : 8 * k + 8, :]

    cot = rowg[0:BLOCKS]
    d_normed = cot * gain
    d_pooled = inverse * (d_normed - jnp.sum(d_normed) / D - normed_out * (jnp.sum(d_normed * normed_out) / D))
    dpo[0:BLOCKS, :] = d_pooled / SEQ
    dcopy = send(dpo, dpp, pair_send.at[4], pair_recv.at[4], partner)
    rowout[...] = rowg
    row_out = pltpu.make_async_copy(rowout, row_ref, local_sem.at[2])
    row_out.start()
    dcopy.wait_recv()
    mine = jnp.concatenate([dpo[pl.ds(3 * c + b, 1), :] for b in range(3)], axis=1)
    theirs = jnp.concatenate([dpp[pl.ds(3 * c + b, 1), :] for b in range(3)], axis=1)

    def weight_block(spot, r):
        at = pl.ds(pl.multiple_of(spot * ROWS + 16 * r, 16), 16)
        return bo[at, :] * mine + bp[at, :] * theirs

    w1 = {}
    for r in range(3):
        for i in SPREAD:
            px, py = shifted(i)
            ws[i, r] = weight_block(px * 4 + py, r).astype(BF16)
        for i in SPREAD:
            w1[i, r] = send(ws.at[i, r], wr.at[i, r], w1_s.at[3 * i + r], w1_r.at[3 * i + r], plane(i))
    for r in range(3):
        wown[r] = weight_block(me, r)
    lane_sum = pm[:, 0:LANE] * dpo[0:1, :]
    for b in range(1, BLOCKS):
        lane_sum += pm[:, b * LANE : (b + 1) * LANE] * dpo[b : b + 1, :]
    gain_in = lax.dot_general(
        jnp.ones((8, LANE), F32), lane_sum, (((1,), (1,)), ((), ())),
        precision=lax.Precision.HIGHEST, preferred_element_type=F32,
    )
    gain_out = cot * normed_out
    for b in range(BLOCKS):
        gs1[b] = gain_in[0:1, b * LANE : (b + 1) * LANE]
        gs1[BLOCKS + b] = gain_out[b : b + 1, :]
    gcopy = send(gs1, gs1p, pair_send.at[5], pair_recv.at[5], partner)
    gcopy.wait_recv()
    g3r[...] = gs1[...] + gs1p[...]
    g1 = []
    for i in PLANE:
        px, py = shifted(i)
        g1.append(send(g3r.at[px * 4 + py], gr1.at[i], g1_s.at[i], g1_r.at[i], plane(i)))

    near_z = [lax.rem(zl + d, 4) for d in range(4)]

    def cube(d):
        return device(zh * 4 + near_z[d], x, y, c)

    def cubes(d):
        return along(4 * d)

    def piece(spot, r):
        return half.at[pl.ds(pl.multiple_of(spot * ROWS + 16 * r, 16), 16), :]

    def placed(spot, r):
        rows = pl.ds(pl.multiple_of(spot * ROWS + 16 * r, 16), 16)
        return grad_ref.at[rows, pl.ds(pl.multiple_of(c * HALF, LANE), HALF)]

    def second(r):
        d = lax.rem(r + 4 - zl, 4)
        return pltpu.make_async_remote_copy(
            src_ref=s2.at[r], dst_ref=s2r.at[d], send_sem=w2_s.at[r], recv_sem=w2_r.at[d],
            device_id=device(zh * 4 + r, x, y, c), device_id_type=MESH,
        )

    def landed(d):
        return pltpu.make_async_remote_copy(
            src_ref=s2r.at[d], dst_ref=s2r.at[d], send_sem=w2_s.at[0], recv_sem=w2_r.at[d],
            device_id=cube(d), device_id_type=MESH,
        )

    def across(d):
        return pltpu.make_async_remote_copy(
            src_ref=s3r.at[zh], dst_ref=s3r.at[zh], send_sem=w3_s.at[d], recv_sem=w3_r.at[d],
            device_id=cubes(d), device_id_type=MESH,
        )

    def fourth(d, r):
        return pltpu.make_async_remote_copy(
            src_ref=piece(me, r), dst_ref=piece(me, r), send_sem=w4_s.at[d], recv_sem=w4_r.at[r],
            device_id=cube(d), device_id_type=MESH,
        )

    def start_across(r):
        for d in range(1, 4):
            landed(d).wait_recv()
        s3r[zh] = s2[r] + s2r[1] + s2r[2] + s2r[3]
        for d in range(1, 4):
            across(d).start()

    def end_across(r):
        for d in range(1, 4):
            across(d).wait_recv()
        whole = s3r[0] + s3r[1] + s3r[2] + s3r[3]
        piece(me, r)[...] = whole.astype(BF16)
        for d in range(1, 4):
            fourth(d, r).start()

    for r in range(3):
        for i in PLANE:
            w1[i, r].wait_recv()
        total = wown[r]
        for i in range(1, NP):
            total += wr[i, r].astype(F32)
        s2[r] = total
        pl.when(zl != r)(lambda r=r: second(r).start())
        if r == 1:
            pl.when(zl == 0)(lambda: start_across(0))
    pl.when(zl == 1)(lambda: start_across(1))
    for copy in g1:
        copy.wait_recv()
    gsum = g3r[me]
    for i in range(1, NP):
        gsum += gr1[i]
    g2r[zl] = gsum
    g2 = [send(g2r.at[zl], g2r.at[zl], g2_s.at[d], g2_r.at[d], cube(d)) for d in range(1, 4)]
    pl.when(zl == 2)(lambda: start_across(2))
    for copy in g2:
        copy.wait_recv()
    g2r[4 + zh] = g2r[0] + g2r[1] + g2r[2] + g2r[3]
    g3 = [send(g2r.at[4 + zh], g2r.at[4 + zh], g3_s.at[d], g3_r.at[d], cubes(d)) for d in range(1, 4)]

    for copy in [*zgather.values(), *relays, *pair, *xgather.values(), *xreduce.values(), *zreduce, dcopy, *w1.values(), gcopy, *g1, *g2]:
        copy.wait_send()

    w5, w6 = {}, []
    for r in range(3):
        pl.when(zl == r)(lambda r=r: end_across(r))
        pl.when(zl != r)(lambda r=r: fourth(1, r).wait_recv())
        for i in SPREAD:
            w5[i, r] = send(piece(me, r), piece(me, r), w5_s.at[3 * i + r], w5_r.at[3 * i + r], plane(i))
        w6.append(send(piece(me, r), placed(me, r), w6_s.at[r], w6_r.at[r], partner))
    for copy in g3:
        copy.wait_recv()
    gfin[me] = g2r[4] + g2r[5] + g2r[6] + g2r[7]
    g5 = [send(gfin.at[me], gfin.at[me], g5_s.at[i], g5_r.at[i], plane(i)) for i in SPREAD]
    for copy in g3:
        copy.wait_send()
    for r in range(3):
        pl.when(zl != r)(lambda r=r: second(r).wait_send())

    def sent():
        for d in range(1, 4):
            across(d).wait_send()
            fourth(d, 0).wait_send()

    pl.when(zl < 3)(sent)
    for r in range(3):
        for i in SPREAD:
            w5[i, r].wait_recv()
            px, py = shifted(back(i))
            spot = px * 4 + py
            w6.append(send(piece(spot, r), placed(spot, r), w6_s.at[3 * i + r], w6_r.at[3 * i + r], partner))
    own_half = pltpu.make_async_copy(half, grad_ref.at[:, pl.ds(pl.multiple_of(c * HALF, LANE), HALF)], local_sem.at[0])
    own_half.start()
    for copy in g5:
        copy.wait_recv()
    gains_out = pltpu.make_async_copy(gfin, gain_ref, local_sem.at[1])
    gains_out.start()
    for copy in [*w5.values(), *g5]:
        copy.wait_send()
    for copy in (own_half, gains_out, row_out):
        copy.wait()
    for copy in w6:
        copy.wait()


def widen(grad_ref, row_ref, gain_ref, row_out, wide_ref, gain_out, grad, wide, row, gain, rowv, gainv, in_sem, out_sem):
    quarter = D // 4
    at = [pl.ds(q * quarter, quarter) for q in range(4)]
    reads = [pltpu.make_async_copy(grad_ref.at[at[q], :], grad.at[at[q], :], in_sem.at[q]) for q in range(4)]
    reads += [pltpu.make_async_copy(row_ref, rowv, in_sem.at[4]), pltpu.make_async_copy(gain_ref, gainv, in_sem.at[5])]
    for copy in reads:
        copy.start()
    writes = []
    for q in range(4):
        reads[q].wait()
        wide[at[q], :] = grad[at[q], :].astype(F32)
        writes.append(pltpu.make_async_copy(wide.at[at[q], :], wide_ref.at[at[q], :], out_sem.at[q]))
        writes[-1].start()
    reads[4].wait()
    reads[5].wait()
    for b in range(BLOCKS):
        cols = slice(b * LANE, (b + 1) * LANE)
        row[:, cols] = rowv[b : b + 1, :]
        gain[0:1, cols] = gainv[b]
        gain[1:2, cols] = gainv[BLOCKS + b]
    writes += [pltpu.make_async_copy(row, row_out, out_sem.at[4]), pltpu.make_async_copy(gain, gain_out, out_sem.at[5])]
    for copy in writes[4:]:
        copy.start()
    for copy in writes:
        copy.wait()


def shards(tokens, norm_gains, enc_weight, head_weight, head_bias, positives):
    vmem, dma = pltpu.VMEM, pltpu.SemaphoreType.DMA
    anywhere = pl.BlockSpec(memory_space=pl.ANY)
    scratch = [
        vmem((1, SEQ, D), BF16),
        vmem((2, D), F32),
        vmem((D, D), BF16),
        vmem((1, 8), jnp.int32),
        vmem((2, SHARD, D), BF16),
        vmem((SHARD,), BF16),
        vmem((SHARD,), BF16),
        vmem((SEQ, D), BF16),
        vmem((2, 2, SEQ, HALF), BF16),
        vmem((SEQ, D), BF16),
        vmem((2, SEQ, HALF), BF16),
        vmem((D, HALF), F32),
        vmem((D, HALF), F32),
        vmem((D, D), F32),
        vmem((SEQ, D), F32),
        vmem((8, LANE), F32),
        vmem((8, LANE), F32),
        vmem((8, LANE), F32),
        vmem((NZ, 8, LANE), BF16),
        vmem((NZ * 8, LANE), F32),
        vmem((NP, 2, 8, D + LANE), BF16),
        vmem((NP, 2, 8, D), BF16),
        vmem((NP, 2, 8, D), BF16),
        vmem((2, 8, D), F32),
        vmem((NZ * 8, LANE), F32),
        vmem((NZ * 8, LANE), F32),
        vmem((8, LANE), F32),
        vmem((8, LANE), F32),
        vmem((NP, 3, 16, HALF), BF16),
        vmem((NP, 3, 16, HALF), BF16),
        vmem((3, 16, HALF), F32),
        vmem((NP, 1, LANE), F32),
        vmem((NP, 1, LANE), F32),
        vmem((NP, 1, LANE), F32),
        vmem((3, 16, HALF), F32),
        vmem((4, 16, HALF), F32),
        vmem((4, 16, HALF), F32),
        vmem((8, 1, LANE), F32),
        vmem((NP, 1, LANE), F32),
        vmem((NP, 1, LANE), F32),
        vmem((D, HALF), BF16),
        vmem((8, LANE), F32),
        dma((6,)),
        dma((6,)), dma((6,)),
        dma((NZ,)), dma((NZ,)),
        dma((2 * NP,)), dma((2 * NP,)),
        dma((2 * NP,)), dma((2 * NP,)),
        dma((NZ,)), dma((NZ,)),
        dma((3 * NP,)), dma((3 * NP,)),
        dma((NP,)), dma((NP,)),
        dma((4,)), dma((4,)),
        dma((4,)), dma((4,)),
        dma((4,)), dma((4,)),
        dma((4,)), dma((4,)),
        dma((4,)), dma((4,)),
        dma((3 * NP,)), dma((3 * NP,)),
        dma((NP,)), dma((NP,)),
        dma((3 * NP,)), dma((3 * NP,)),
    ]
    row_part, grad, gain_part = pl.pallas_call(
        kernel,
        out_shape=(
            jax.ShapeDtypeStruct((8, LANE), F32),
            jax.ShapeDtypeStruct((D, D), BF16),
            jax.ShapeDtypeStruct((NP, 1, LANE), F32),
        ),
        in_specs=[anywhere] * 6,
        out_specs=(anywhere,) * 3,
        scratch_shapes=scratch,
        compiler_params=pltpu.CompilerParams(collective_id=0, has_side_effects=True),
    )(tokens, norm_gains, enc_weight, head_weight, head_bias, positives)
    return pl.pallas_call(
        widen,
        out_shape=tuple(jax.ShapeDtypeStruct((rows, D), F32) for rows in (1, D, 2)),
        in_specs=[anywhere] * 3,
        out_specs=(anywhere,) * 3,
        scratch_shapes=[
            vmem((D, D), BF16), vmem((D, D), F32), vmem((1, D), F32), vmem((2, D), F32),
            vmem((8, LANE), F32), vmem((NP, 1, LANE), F32), dma((6,)), dma((6,)),
        ],
    )(grad, row_part, gain_part)


def solution(mesh):
    placed = (P(("label", "doc"), None, None), P(), P(), P(("label", "doc"), None), P(("label", "doc")), P(("label", "doc"), None))
    return jax.shard_map(
        shards, mesh=mesh, in_specs=placed, out_specs=(P(("label", "doc"), None), P(), P()), check_vma=False
    )
```

```python
import math

import jax
import jax.numpy as jnp
from jax import lax
from jax.experimental import pallas as pl
from jax.experimental.pallas import tpu as pltpu
from jax.sharding import PartitionSpec as P

D, SEQ, SHARD = 768, 128, 512
NZ, NX, NY, NP = 16, 4, 4, 16
LANE, HALF, ROWS = 128, 384, 48
BLOCKS = D // LANE
EPSILON = 1e-05
BF16, F32 = jnp.bfloat16, jnp.float32
MESH = pl.DeviceIdType.MESH
ROOT = math.sqrt(2.0 / math.pi)
STEP = (0, 1, 2, 3, 4, 13, 14, 15, 5, 6, 7, 8, 9, 10, 11, 12)
FAR_FIRST = (11, 10, 12, 9, 13, 8, 14, 15, 4, 3, 5, 2, 6, 1, 7)
SPREAD = (1, 4, 12, 3, 5, 13, 8, 2, 7, 15, 9, 6, 14, 11, 10)
WITHIN_4 = (15, 4, 5, 3, 6, 2, 7, 1)
RELAYS = ((1, 4, 8, 4), (5, 3, 12, 12))
PAIRS = ((0, 1), (3, 2))
PLANE = tuple(4 * dx + dy for pair in PAIRS for dx in pair for dy in (1, 3, 2, 0) if dx or dy)


def device(z, x, y, c):
    return (z * 4 + lax.div(x, 2) * 2 + c, y * 2 + lax.rem(x, 2))


def contract(a, b, dims):
    return lax.dot_general(a, b, ((dims[:1], dims[1:]), ((), ())), preferred_element_type=F32)


def high_low(v):
    high = v.astype(BF16)
    return high, (v - high.astype(F32)).astype(BF16)


def kernel(
    tok_hbm, gains_hbm, enc_hbm, head_hbm, bias_hbm, pos_hbm,
    row_ref, grad_ref, gain_ref,
    tok_ref, gains_ref, enc_ref, pos_ref, head, bias0, bias1, act, gel, product, bq, bg, pm, nrm, r8, g8, zs, zbuf, zf, xbuf,
    rs, rr, rown, rz, rzr, dpo, dpg, ws, wr, wown, gs1, gs1p, gr1, s2, s2r, s3r, g2r, g3r, gfin, half, rowout,
    local_sem, pair_send, pair_recv, bq_s, bq_r, dp_s, dp_r, za_s, za_r, xa_s, xa_r, xr_s, xr_r, zr_s, zr_r,
    w1_s, w1_r, g1_s, g1_r, w2_s, w2_r, g2_s, g2_r, w3_s, w3_r, g3_s, g3_r,
    w4_s, w4_r, w5_s, w5_r, g5_s, g5_r, w6_s, w6_r,
):
    label, doc = lax.axis_index("label"), lax.axis_index("doc")
    z, c = lax.div(label, 4), lax.rem(label, 2)
    x, y = lax.rem(lax.div(label, 2), 2) * 2 + lax.rem(doc, 2), lax.div(doc, 2)
    zh, zl = lax.div(z, 4), lax.rem(z, 4)
    me = x * 4 + y
    partner = device(z, x, y, 1 - c)

    def along(k):
        return device(lax.rem(z + k, NZ), x, y, c)

    def shifted(i):
        return lax.rem(x + i // 4, NX), lax.rem(y + i % 4, NY)

    def plane(i):
        return device(z, *shifted(i), c)

    def back(i):
        return (4 - i // 4) % 4 * 4 + (4 - i % 4) % 4

    def send(src, dst, send_sem, recv_sem, to):
        copy = pltpu.make_async_remote_copy(
            src_ref=src, dst_ref=dst, send_sem=send_sem, recv_sem=recv_sem, device_id=to, device_id_type=MESH
        )
        copy.start()
        return copy

    local = [
        pltpu.make_async_copy(src, dst, local_sem.at[n])
        for n, (src, dst) in enumerate((
            (tok_hbm, tok_ref), (gains_hbm, gains_ref), (enc_hbm, enc_ref), (pos_hbm, pos_ref),
            (head_hbm, head.at[0]), (bias_hbm, bias0),
        ))
    ]
    for copy in local[:4]:
        copy.start()
    def line(n):
        return lax.rem(y + n // 2, NY), (1 - c if n % 2 else c)

    def in_line(n):
        return device(z, x, *line(n))

    barrier = pltpu.get_barrier_semaphore()
    for to in [in_line(n) for n in (1, 3, 5, 7)] + [along(STEP[k]) for k in WITHIN_4] + [plane(i) for i in PLANE]:
        pl.semaphore_signal(barrier, inc=1, device_id=to, device_id_type=MESH)

    for copy in local[4:]:
        copy.start()

    local[0].wait()
    local[1].wait()
    tok = tok_ref[0].astype(F32)
    center = tok - jnp.mean(tok, axis=-1, keepdims=True)
    normed = center * lax.rsqrt(jnp.mean(center * center, axis=-1, keepdims=True) + EPSILON)
    nrm[...] = normed
    act[...] = (normed * gains_ref[0:1, :]).astype(BF16)
    local[2].wait()
    pre = jnp.dot(act[...], enc_ref[...], preferred_element_type=F32)
    tanh = jnp.tanh(ROOT * (pre + 0.044715 * (pre * pre * pre)))
    cdf = 0.5 * (1.0 + tanh)
    pooled = jnp.mean(tok + pre * cdf, axis=0, keepdims=True)
    for b in range(BLOCKS):
        r8[b : b + 1, :] = pooled[:, b * LANE : (b + 1) * LANE]
        g8[b : b + 1, :] = gains_ref[1:2, b * LANE : (b + 1) * LANE]
    pooled = r8[0:BLOCKS, :]
    gain = g8[0:BLOCKS, :]
    center = pooled - jnp.sum(pooled) / D
    inverse = lax.rsqrt(jnp.sum(center * center, keepdims=True) / D + EPSILON)
    normed_out = center * inverse
    zs[...] = jnp.zeros_like(zs)
    zs[0:BLOCKS, :] = normed_out * gain
    local[3].wait()
    ids = pos_ref[...]
    zs[6:7, 0:8] = (jnp.where(ids < 0, 512, jnp.right_shift(ids, 9)) - 256).astype(F32)
    zs[7:8, 0:8] = (jnp.bitwise_and(ids, 511) - 256).astype(F32)
    zbuf[0] = zs[...].astype(BF16)

    pl.semaphore_wait(barrier, 27)
    zgather = {k: send(zbuf.at[0], zbuf.at[k], za_s.at[k], za_r.at[k], along(STEP[k])) for k in WITHIN_4}
    pair = [
        send(head_hbm, head.at[1], pair_send.at[0], pair_recv.at[0], partner),
        send(bias_hbm, bias1, pair_send.at[1], pair_recv.at[1], partner),
    ]

    slope = cdf + (0.5 * ROOT) * pre * (1.0 - tanh * tanh) * (1.0 + 0.134145 * (pre * pre))
    high, low = high_low(slope)
    for h in range(2):
        gel[h, 0] = high[:, h * HALF : (h + 1) * HALF]
        gel[h, 1] = low[:, h * HALF : (h + 1) * HALF]
    for h in range(2):
        for q in range(3):
            cols = slice(q * 256, (q + 1) * 256)
            product[cols, :] = contract(act[:, cols], gel[h, 0], (0, 0)) + contract(act[:, cols], gel[h, 1], (0, 0))
        for spot in range(NP):
            strip = product[spot * ROWS : (spot + 1) * ROWS, :].astype(BF16)
            for r in range(3):
                bq[h, spot % 4, spot // 4, r] = strip[16 * r : 16 * r + 16]

    def exchange(n):
        to_y, to_c = line(n)
        return send(bq.at[to_c, to_y], bg.at[n], bq_s.at[n], bq_r.at[n], in_line(n))

    products = [exchange(n) for n in (4, 5, 1)]
    for q in range(3):
        cols = slice(q * 256, (q + 1) * 256)
        n_high, n_low = high_low(nrm[:, cols])
        for h in range(2):
            block = contract(n_high, gel[h, 0], (0, 0)) + contract(n_low, gel[h, 0], (0, 0)) + contract(n_high, gel[h, 1], (0, 0))
            pm[cols, h * HALF : (h + 1) * HALF] = block * enc_ref[cols, h * HALF : (h + 1) * HALF].astype(F32)
    for ref in (rz, dpo, gs1):
        ref[...] = jnp.zeros_like(ref)

    relays = []
    for n, (first, count, slot, step) in enumerate(RELAYS):
        for k in range(first, first + count):
            zgather[k].wait_recv()
        relays.append(
            send(zbuf.at[pl.ds(first, count)], zbuf.at[pl.ds(slot, count)], za_s.at[8 + n], za_r.at[8 + n], along(step))
        )
    xgather = {}
    for h in range(2):
        if h:
            for copy in [zgather[15], *relays]:
                copy.wait_recv()
        zf[64 * h : 64 * h + 64, :] = zbuf[8 * h : 8 * h + 8].reshape(64, LANE).astype(F32)
        for b in range(BLOCKS):
            xbuf[0, h, :, b * LANE : (b + 1) * LANE] = zf[pl.ds(64 * h + b, 8, stride=8), :].astype(BF16)
        first, second = zf[pl.ds(64 * h + 6, 8, stride=8), :], zf[pl.ds(64 * h + 7, 8, stride=8), :]
        lanes = lax.broadcasted_iota(jnp.int32, (8, LANE), 1)
        xbuf[0, h, :, D:] = jnp.where(lanes < 8, first, pltpu.roll(second, 8, 1)).astype(BF16)
        for i in PLANE:
            at = 2 * i + h
            xgather[i, h] = send(xbuf.at[0, h], xbuf.at[i, h], xa_s.at[at], xa_r.at[at], plane(i))

    local[4].wait()
    local[5].wait()
    for copy in pair:
        copy.wait_recv()

    flat = label * 8 + doc
    bases = (flat * SHARD, (flat + (1 - 2 * c) * 8) * SHARD)
    spots = lax.broadcasted_iota(jnp.int32, (64, SHARD), 1)
    xreduce = {}
    for h, columns in [(h, columns) for h in range(2) for columns in PAIRS]:
        slots = [4 * dx + dy for dx in columns for dy in range(4)]
        for i in slots:
            if i:
                xgather[i, h].wait_recv()
        block = jnp.concatenate([xbuf[4 * dx : 4 * dx + 4, h].reshape(32, D + LANE) for dx in columns], axis=0)
        embed = block[:, 0:D]
        code = block[:, D:].astype(F32)
        ids = ((code + 256.0) * 512.0 + (pltpu.roll(code, LANE - 8, 1) + 256.0)).astype(jnp.int32)
        total = jnp.zeros((64, D), F32)
        for s in range(2):
            logits = contract(embed, head[s], (1, 1)) + (bias0, bias1)[s][...].astype(F32).reshape(1, SHARD)
            near = ids - bases[s]
            target = near[:, 0:1] == spots
            for q in range(1, 8):
                target = jnp.logical_or(target, near[:, q : q + 1] == spots)
            d_logit = (jax.nn.sigmoid(logits) - target.astype(F32)).astype(BF16)
            total += jnp.dot(d_logit, head[s], preferred_element_type=F32)
        for m, i in enumerate(slots):
            part = total[8 * m : 8 * m + 8]
            if i:
                rs[i, h] = part.astype(BF16)
            else:
                rown[h] = part
        for i in slots:
            if i:
                at = 2 * i + h
                xreduce[i, h] = send(rs.at[i, h], rr.at[i, h], xr_s.at[at], xr_r.at[at], plane(back(i)))
    zreduce = []
    for h in range(2):
        for i in PLANE:
            xreduce[i, h].wait_recv()
        total = rown[h]
        for i in range(1, NP):
            total += rr[i, h].astype(F32)
        for b in range(BLOCKS):
            rz[pl.ds(64 * h + b, 8, stride=8), :] = total[:, b * LANE : (b + 1) * LANE]
        for k in FAR_FIRST:
            if k // 8 == h:
                at = pl.ds(8 * k, 8)
                zreduce.append(send(rz.at[at, :], rzr.at[at, :], zr_s.at[k], zr_r.at[k], along(NZ - STEP[k])))
    products += [exchange(n) for n in (2, 6, 3, 7)]
    for copy in zreduce:
        copy.wait_recv()
    rowg = rz[0:8, :]
    for k in range(1, NZ):
        rowg += rzr[8 * k : 8 * k + 8, :]

    cot = rowg[0:BLOCKS]
    d_normed = cot * gain
    d_pooled = inverse * (d_normed - jnp.sum(d_normed) / D - normed_out * (jnp.sum(d_normed * normed_out) / D))
    dpo[0:BLOCKS, :] = d_pooled / SEQ
    dcopies = [send(dpo, dpg.at[n], dp_s.at[n], dp_r.at[n], in_line(n)) for n in (4, 5, 2, 6, 3, 7, 1)]
    rowout[...] = rowg
    row_out = pltpu.make_async_copy(rowout, row_ref, local_sem.at[2])
    row_out.start()
    for copy in [*products, *dcopies]:
        copy.wait_recv()
    dpg[0] = dpo[...]
    scales = [jnp.concatenate([dpg[n, pl.ds(3 * c + b, 1), :] for b in range(3)], axis=1) for n in range(8)]

    def weight_block(to_x, r):
        total = bq[c, y, to_x, r].astype(F32) * scales[0]
        for n in range(1, 8):
            total += bg[n, to_x, r].astype(F32) * scales[n]
        return total

    w1 = {}
    for r in range(3):
        for dx in (2, 1, 3):
            ws[dx, r] = weight_block(lax.rem(x + dx, NX), r)
        for dx in (2, 1, 3):
            w1[dx, r] = send(ws.at[dx, r], wr.at[dx, r], w1_s.at[3 * dx + r], w1_r.at[3 * dx + r], plane(4 * dx))
    for r in range(3):
        wown[r] = weight_block(x, r)
    lane_sum = pm[:, 0:LANE] * dpo[0:1, :]
    for b in range(1, BLOCKS):
        lane_sum += pm[:, b * LANE : (b + 1) * LANE] * dpo[b : b + 1, :]
    gain_in = lax.dot_general(
        jnp.ones((8, LANE), F32), lane_sum, (((1,), (1,)), ((), ())),
        precision=lax.Precision.HIGHEST, preferred_element_type=F32,
    )
    gain_out = cot * normed_out
    for b in range(BLOCKS):
        gs1[b] = gain_in[0:1, b * LANE : (b + 1) * LANE]
        gs1[BLOCKS + b] = gain_out[b : b + 1, :]
    gcopy = send(gs1, gs1p, pair_send.at[5], pair_recv.at[5], partner)
    gcopy.wait_recv()
    g3r[...] = gs1[...] + gs1p[...]
    g1 = []
    for i in PLANE:
        px, py = shifted(i)
        g1.append(send(g3r.at[px * 4 + py], gr1.at[i], g1_s.at[i], g1_r.at[i], plane(i)))

    near_z = [lax.rem(zl + d, 4) for d in range(4)]

    def cube(d):
        return device(zh * 4 + near_z[d], x, y, c)

    def cubes(d):
        return along(4 * d)

    def piece(spot, r):
        return half.at[pl.ds(pl.multiple_of(spot * ROWS + 16 * r, 16), 16), :]

    def placed(spot, r):
        rows = pl.ds(pl.multiple_of(spot * ROWS + 16 * r, 16), 16)
        return grad_ref.at[rows, pl.ds(pl.multiple_of(c * HALF, LANE), HALF)]

    def second(r):
        d = lax.rem(r + 4 - zl, 4)
        return pltpu.make_async_remote_copy(
            src_ref=s2.at[r], dst_ref=s2r.at[d], send_sem=w2_s.at[r], recv_sem=w2_r.at[d],
            device_id=device(zh * 4 + r, x, y, c), device_id_type=MESH,
        )

    def landed(d):
        return pltpu.make_async_remote_copy(
            src_ref=s2r.at[d], dst_ref=s2r.at[d], send_sem=w2_s.at[0], recv_sem=w2_r.at[d],
            device_id=cube(d), device_id_type=MESH,
        )

    def across(d):
        return pltpu.make_async_remote_copy(
            src_ref=s3r.at[zh], dst_ref=s3r.at[zh], send_sem=w3_s.at[d], recv_sem=w3_r.at[d],
            device_id=cubes(d), device_id_type=MESH,
        )

    def fourth(d, r):
        return pltpu.make_async_remote_copy(
            src_ref=piece(me, r), dst_ref=piece(me, r), send_sem=w4_s.at[d], recv_sem=w4_r.at[r],
            device_id=cube(d), device_id_type=MESH,
        )

    def start_across(r):
        for d in range(1, 4):
            landed(d).wait_recv()
        s3r[zh] = s2[r] + s2r[1] + s2r[2] + s2r[3]
        for d in range(1, 4):
            across(d).start()

    def end_across(r):
        for d in range(1, 4):
            across(d).wait_recv()
        whole = s3r[0] + s3r[1] + s3r[2] + s3r[3]
        piece(me, r)[...] = whole.astype(BF16)
        for d in range(1, 4):
            fourth(d, r).start()

    for r in range(3):
        for dx in (1, 3, 2):
            w1[dx, r].wait_recv()
        s2[r] = wown[r] + wr[1, r] + wr[2, r] + wr[3, r]
        pl.when(zl != r)(lambda r=r: second(r).start())
        if r == 1:
            pl.when(zl == 0)(lambda: start_across(0))
    pl.when(zl == 1)(lambda: start_across(1))
    for copy in g1:
        copy.wait_recv()
    gsum = g3r[me]
    for i in range(1, NP):
        gsum += gr1[i]
    g2r[zl] = gsum
    g2 = [send(g2r.at[zl], g2r.at[zl], g2_s.at[d], g2_r.at[d], cube(d)) for d in range(1, 4)]
    pl.when(zl == 2)(lambda: start_across(2))
    for copy in g2:
        copy.wait_recv()
    g2r[4 + zh] = g2r[0] + g2r[1] + g2r[2] + g2r[3]
    g3 = [send(g2r.at[4 + zh], g2r.at[4 + zh], g3_s.at[d], g3_r.at[d], cubes(d)) for d in range(1, 4)]

    for copy in [*zgather.values(), *relays, *pair, *xgather.values(), *xreduce.values(), *zreduce, *products, *dcopies, *w1.values(), gcopy, *g1, *g2]:
        copy.wait_send()

    w5, w6 = {}, []
    for r in range(3):
        pl.when(zl == r)(lambda r=r: end_across(r))
        pl.when(zl != r)(lambda r=r: fourth(1, r).wait_recv())
        for i in SPREAD:
            w5[i, r] = send(piece(me, r), piece(me, r), w5_s.at[3 * i + r], w5_r.at[3 * i + r], plane(i))
        w6.append(send(piece(me, r), placed(me, r), w6_s.at[r], w6_r.at[r], partner))
    for copy in g3:
        copy.wait_recv()
    gfin[me] = g2r[4] + g2r[5] + g2r[6] + g2r[7]
    g5 = [send(gfin.at[me], gfin.at[me], g5_s.at[i], g5_r.at[i], plane(i)) for i in SPREAD]
    for copy in g3:
        copy.wait_send()
    for r in range(3):
        pl.when(zl != r)(lambda r=r: second(r).wait_send())

    def sent():
        for d in range(1, 4):
            across(d).wait_send()
            fourth(d, 0).wait_send()

    pl.when(zl < 3)(sent)
    for r in range(3):
        for i in SPREAD:
            w5[i, r].wait_recv()
            px, py = shifted(back(i))
            spot = px * 4 + py
            w6.append(send(piece(spot, r), placed(spot, r), w6_s.at[3 * i + r], w6_r.at[3 * i + r], partner))
    own_half = pltpu.make_async_copy(half, grad_ref.at[:, pl.ds(pl.multiple_of(c * HALF, LANE), HALF)], local_sem.at[0])
    own_half.start()
    for copy in g5:
        copy.wait_recv()
    gains_out = pltpu.make_async_copy(gfin, gain_ref, local_sem.at[1])
    gains_out.start()
    for copy in [*w5.values(), *g5]:
        copy.wait_send()
    for copy in (own_half, gains_out, row_out):
        copy.wait()
    for copy in w6:
        copy.wait()


def widen(grad_ref, row_ref, gain_ref, row_out, wide_ref, gain_out, grad, wide, row, gain, rowv, gainv, in_sem, out_sem):
    quarter = D // 4
    at = [pl.ds(q * quarter, quarter) for q in range(4)]
    reads = [pltpu.make_async_copy(grad_ref.at[at[q], :], grad.at[at[q], :], in_sem.at[q]) for q in range(4)]
    reads += [pltpu.make_async_copy(row_ref, rowv, in_sem.at[4]), pltpu.make_async_copy(gain_ref, gainv, in_sem.at[5])]
    for copy in reads:
        copy.start()
    writes = []
    for q in range(4):
        reads[q].wait()
        wide[at[q], :] = grad[at[q], :].astype(F32)
        writes.append(pltpu.make_async_copy(wide.at[at[q], :], wide_ref.at[at[q], :], out_sem.at[q]))
        writes[-1].start()
    reads[4].wait()
    reads[5].wait()
    for b in range(BLOCKS):
        cols = slice(b * LANE, (b + 1) * LANE)
        row[:, cols] = rowv[b : b + 1, :]
        gain[0:1, cols] = gainv[b]
        gain[1:2, cols] = gainv[BLOCKS + b]
    writes += [pltpu.make_async_copy(row, row_out, out_sem.at[4]), pltpu.make_async_copy(gain, gain_out, out_sem.at[5])]
    for copy in writes[4:]:
        copy.start()
    for copy in writes:
        copy.wait()


def shards(tokens, norm_gains, enc_weight, head_weight, head_bias, positives):
    vmem, dma = pltpu.VMEM, pltpu.SemaphoreType.DMA
    anywhere = pl.BlockSpec(memory_space=pl.ANY)
    scratch = [
        vmem((1, SEQ, D), BF16),
        vmem((2, D), F32),
        vmem((D, D), BF16),
        vmem((1, 8), jnp.int32),
        vmem((2, SHARD, D), BF16),
        vmem((SHARD,), BF16),
        vmem((SHARD,), BF16),
        vmem((SEQ, D), BF16),
        vmem((2, 2, SEQ, HALF), BF16),
        vmem((D, HALF), F32),
        vmem((2, NY, NX, 3, 16, HALF), BF16),
        vmem((8, NX, 3, 16, HALF), BF16),
        vmem((D, D), F32),
        vmem((SEQ, D), F32),
        vmem((8, LANE), F32),
        vmem((8, LANE), F32),
        vmem((8, LANE), F32),
        vmem((NZ, 8, LANE), BF16),
        vmem((NZ * 8, LANE), F32),
        vmem((NP, 2, 8, D + LANE), BF16),
        vmem((NP, 2, 8, D), BF16),
        vmem((NP, 2, 8, D), BF16),
        vmem((2, 8, D), F32),
        vmem((NZ * 8, LANE), F32),
        vmem((NZ * 8, LANE), F32),
        vmem((8, LANE), F32),
        vmem((8, 8, LANE), F32),
        vmem((NX, 3, 16, HALF), F32),
        vmem((NX, 3, 16, HALF), F32),
        vmem((3, 16, HALF), F32),
        vmem((NP, 1, LANE), F32),
        vmem((NP, 1, LANE), F32),
        vmem((NP, 1, LANE), F32),
        vmem((3, 16, HALF), F32),
        vmem((4, 16, HALF), F32),
        vmem((4, 16, HALF), F32),
        vmem((8, 1, LANE), F32),
        vmem((NP, 1, LANE), F32),
        vmem((NP, 1, LANE), F32),
        vmem((D, HALF), BF16),
        vmem((8, LANE), F32),
        dma((6,)),
        dma((6,)), dma((6,)),
        dma((8,)), dma((8,)),
        dma((8,)), dma((8,)),
        dma((NZ,)), dma((NZ,)),
        dma((2 * NP,)), dma((2 * NP,)),
        dma((2 * NP,)), dma((2 * NP,)),
        dma((NZ,)), dma((NZ,)),
        dma((3 * NX,)), dma((3 * NX,)),
        dma((NP,)), dma((NP,)),
        dma((4,)), dma((4,)),
        dma((4,)), dma((4,)),
        dma((4,)), dma((4,)),
        dma((4,)), dma((4,)),
        dma((4,)), dma((4,)),
        dma((3 * NP,)), dma((3 * NP,)),
        dma((NP,)), dma((NP,)),
        dma((3 * NP,)), dma((3 * NP,)),
    ]
    row_part, grad, gain_part = pl.pallas_call(
        kernel,
        out_shape=(
            jax.ShapeDtypeStruct((8, LANE), F32),
            jax.ShapeDtypeStruct((D, D), BF16),
            jax.ShapeDtypeStruct((NP, 1, LANE), F32),
        ),
        in_specs=[anywhere] * 6,
        out_specs=(anywhere,) * 3,
        scratch_shapes=scratch,
        compiler_params=pltpu.CompilerParams(collective_id=0, has_side_effects=True),
    )(tokens, norm_gains, enc_weight, head_weight, head_bias, positives)
    return pl.pallas_call(
        widen,
        out_shape=tuple(jax.ShapeDtypeStruct((rows, D), F32) for rows in (1, D, 2)),
        in_specs=[anywhere] * 3,
        out_specs=(anywhere,) * 3,
        scratch_shapes=[
            vmem((D, D), BF16), vmem((D, D), F32), vmem((1, D), F32), vmem((2, D), F32),
            vmem((8, LANE), F32), vmem((NP, 1, LANE), F32), dma((6,)), dma((6,)),
        ],
    )(grad, row_part, gain_part)


def solution(mesh):
    placed = (P(("label", "doc"), None, None), P(), P(), P(("label", "doc"), None), P(("label", "doc")), P(("label", "doc"), None))
    return jax.shard_map(
        shards, mesh=mesh, in_specs=placed, out_specs=(P(("label", "doc"), None), P(), P()), check_vma=False
    )
```
